128 devices in a mesh: slab: 8 (over x, y_hi), tile: 16 (over y_lo, z, core).
Axes of the slice: x: 4, y: 4 (y_hi: 2, y_lo: 2; y = y_hi * 2 + y_lo), z: 4, core: 2. Of those that a mesh axis runs over, the one named last changes fastest.
Arguments:
- particles: float32 [7, 16, 32, 1536], P(None, 'slab', 'tile')
- counts: int32 [16, 32, 48], P('slab', 'tile'), may hold values from 10 to 32, as said below
- leavers: int32 [2, 8, 32, 48], P(None, 'slab', 'tile'), may hold values from 0 to 4, as said below
Outputs:
- kept: float32 [7, 16, 32, 1536], P(None, 'slab', 'tile')
- arrivals: float32 [2, 7, 24576], P(None, None, ('slab', 'tile'))
The draws below stay inside these ranges and needn't reach their ends.
Inputs may be any that keep to these rules, and one draw needn't show every extreme that they name: `counts`: one cell holds exactly 32. Over the 2 x 48 cells of one face of one device the leavers sum to exactly 192; one face cell of each face has 4.
All inputs are finite; a program needn't handle non-finite values.
Results may differ from the reference program's by a relative error of at most 0.0003.
Values sent between devices are 32-bit elements; how exact they have to be, the bound alone decides.
No kernel may reach another device: no remote copies, remote signals or barrier semaphores. Data moves between devices by JAX's collectives and lax.ppermute only.
A program may use at most 128 MiB of HBM per device.

```python
import math
import jax
import jax.numpy as jnp
from jax import lax

CX = 2
CY = 2
CZ = 48
SLOTS = 32
LMAX = 4
SLABS = 8
TILES = 16
NX = 16
NY = 32
FACE_ROWS = 192


def draw_particles(key, part):
    subkeys = jax.random.split(jax.random.fold_in(key, 11), 3)
    grid_shape = (NX, NY, CZ * SLOTS)
    position = jax.random.uniform(subkeys[0], (3,) + grid_shape, jnp.float32)
    velocity = 0.3 * jnp.clip(jax.random.normal(subkeys[1], (3,) + grid_shape, jnp.float32), -4.0, 4.0)
    density = 1.0 + 0.01 * jnp.clip(jax.random.normal(subkeys[2], (1,) + grid_shape, jnp.float32), -4.0, 4.0)
    return jnp.concatenate([position, velocity, density], axis=0)


def draw_counts(key, part):
    subkeys = jax.random.split(jax.random.fold_in(key, 23), 3)
    grid_shape = (NX, NY, CZ)
    front_x = jax.random.randint(subkeys[0], (), 0, NX - 1)
    column = lax.broadcasted_iota(jnp.int32, grid_shape, 0)
    across = lax.broadcasted_iota(jnp.int32, grid_shape, 1)
    upward = lax.broadcasted_iota(jnp.int32, grid_shape, 2)
    band = (column == front_x) | (column == front_x + 1)
    dense = jax.random.randint(subkeys[1], grid_shape, SLOTS - 4, SLOTS + 1)
    sparse = jax.random.randint(subkeys[2], grid_shape, 5 * SLOTS // 16, 5 * SLOTS // 8 + 1)
    filled = jnp.where(band, dense, sparse)
    anchor = (column == front_x) & (across == 0) & (upward == 0)
    return jnp.where(anchor, SLOTS, filled).astype(jnp.int32)


def draw_leavers(key, part):
    tile_count = NY // CY
    block_count = 2 * SLABS * tile_count
    cell_total = CY * CZ
    pair_total = cell_total // 2
    block_keys = jax.random.split(jax.random.fold_in(key, 37), block_count)

    def one_face(block_key):
        order_key, spread_key = jax.random.split(block_key)
        order = jax.random.permutation(order_key, cell_total)
        spread = jax.random.randint(spread_key, (pair_total,), 0, LMAX // 2 + 1)
        spread = spread.at[0].set(LMAX // 2)
        values = jnp.concatenate([LMAX // 2 + spread, LMAX // 2 - spread]).astype(jnp.int32)
        return jnp.zeros((cell_total,), jnp.int32).at[order].set(values)
    faces = jax.vmap(one_face)(block_keys)
    return faces.reshape(2, SLABS, NY, CZ)


def setup_inputs(seed: int = 0) -> dict:
    key_list = jax.random.split(jax.random.key(seed), 4)
    particles = draw_particles(jax.random.fold_in(key_list[3], 71), 0)
    counts = draw_counts(jax.random.fold_in(key_list[3], 71), 0)
    leavers = draw_leavers(jax.random.fold_in(key_list[3], 71), 0)
    return dict(particles=particles, counts=counts, leavers=leavers)


sound_speed = 10.0
smoothing = 0.5
cell_side = 2.0 * smoothing
kernel_norm = 21.0 / (16.0 * math.pi * smoothing ** 3)
grad_scale = -5.0 * kernel_norm / (smoothing * smoothing)
eos_stiff = sound_speed * sound_speed / 7.0
particle_mass = 0.125
viscosity = 0.1
visc_floor = 0.01 * smoothing * smoothing
time_step = 0.01
gravity = 9.81
layer_block = 4

def occupied(cell_counts):
    filled = jnp.repeat(cell_counts, SLOTS, axis=-1)
    slot_index = jnp.arange(filled.shape[-1], dtype=jnp.int32) % SLOTS
    return (slot_index < filled).astype(jnp.float32)

def pair_rates(center, beside_all):
    span_x, span_y, span_z = (center.shape[1], center.shape[2], center.shape[3])
    dens_c = center[6] + 1.0 - center[7]
    dens_n = beside_all[6] + 1.0 - beside_all[7]
    ratio_c = eos_stiff * (dens_c ** 7 - 1.0) / (dens_c * dens_c)
    ratio_n = eos_stiff * (dens_n ** 7 - 1.0) / (dens_n * dens_n)
    accel_sum = jnp.zeros((3,) + center.shape[1:], jnp.float32)
    drift_sum = jnp.zeros(center.shape[1:], jnp.float32)
    for step_x in range(3):
        for step_y in range(3):
            for step_z in range(3):
                neighbour = beside_all[:, step_x:step_x + span_x, step_y:step_y + span_y, step_z:step_z + span_z]
                near_dens = dens_n[step_x:step_x + span_x, step_y:step_y + span_y, step_z:step_z + span_z]
                near_ratio = ratio_n[step_x:step_x + span_x, step_y:step_y + span_y, step_z:step_z + span_z]
                cell_gap = jnp.array([float(1 - step_x), float(1 - step_y), float(1 - step_z)], jnp.float32).reshape(3, 1, 1, 1, 1, 1) * cell_side
                offset_vec = center[0:3, ..., None] - neighbour[0:3, ..., None, :] + cell_gap
                dist_sq = lax.optimization_barrier(jnp.sum(offset_vec * offset_vec, axis=0))
                support = jnp.maximum(1.0 - jnp.sqrt(dist_sq) / (2.0 * smoothing), 0.0)
                slope_term = grad_scale * support * support * support * neighbour[7][..., None, :]
                approach = lax.optimization_barrier(jnp.sum((center[3:6, ..., None] - neighbour[3:6, ..., None, :]) * offset_vec, axis=0))
                mean_dens = 0.5 * (dens_c[..., None] + near_dens[..., None, :])
                visc_term = -viscosity * sound_speed * smoothing * jnp.minimum(approach, 0.0) / ((dist_sq + visc_floor) * mean_dens)
                force_term = (ratio_c[..., None] + near_ratio[..., None, :] + visc_term) * slope_term
                accel_sum = accel_sum - particle_mass * lax.optimization_barrier(jnp.sum(force_term * offset_vec, axis=-1))
                drift_sum = drift_sum + particle_mass * lax.optimization_barrier(jnp.sum(slope_term * approach, axis=-1))
    gravity_vec = jnp.array([0.0, 0.0, gravity], jnp.float32).reshape(3, 1, 1, 1, 1)
    return jnp.concatenate([accel_sum - gravity_vec, drift_sum[None]], axis=0)

def region_rates(extended):
    span_x = extended.shape[1] - 2
    span_y = extended.shape[2] - 2
    layers = extended.shape[3] // SLOTS
    cells_grid = extended.reshape(8, span_x + 2, span_y + 2, layers, SLOTS)
    padded = jnp.pad(cells_grid, ((0, 0), (0, 0), (0, 0), (1, 1), (0, 0)))

    def one_block(block_index):
        layer_start = (block_index * layer_block).astype(jnp.int32)
        beside_all = lax.dynamic_slice_in_dim(padded, layer_start, layer_block + 2, axis=3)
        return pair_rates(beside_all[:, 1:-1, 1:-1, 1:-1], beside_all)
    stacked = lax.map(one_block, jnp.arange(layers // layer_block, dtype=jnp.int32))
    ordered = jnp.moveaxis(stacked, 0, 3)
    return ordered.reshape(4, span_x, span_y, layers * SLOTS)

def predict(fields, rates_now):
    position = fields[0:3] + 0.5 * time_step * fields[3:6]
    velocity = fields[3:6] + 0.5 * time_step * rates_now[0:3]
    density = fields[6:7] + 0.5 * time_step * rates_now[3:4]
    return jnp.concatenate([position, velocity, density, fields[7:8]], axis=0)

def correct(fields, rates_mid):
    velocity = fields[3:6] + time_step * rates_mid[0:3]
    density = fields[6:7] + time_step * rates_mid[3:4]
    position = fields[0:3] + 0.5 * time_step * (fields[3:6] + velocity)
    return jnp.concatenate([position, velocity, density], axis=0)

def pack_leavers(face_state, face_count, face_leave):
    cell_total = face_count.shape[0] * face_count.shape[1]
    row_total = cell_total * LMAX // 2
    leave_quota = face_leave.reshape(cell_total)
    occupancy = face_count.reshape(cell_total)
    row_ends = jnp.cumsum(leave_quota, dtype=jnp.int32)
    starts = row_ends - leave_quota
    row_ids = jnp.arange(row_total, dtype=jnp.int32)
    owner_mask = (starts[None, :] <= row_ids[:, None]) & (row_ends[None, :] > row_ids[:, None])
    root = jnp.arange(cell_total, dtype=jnp.int32) * SLOTS + occupancy - leave_quota - starts
    source_row = lax.optimization_barrier(jnp.sum(jnp.where(owner_mask, root[None, :], 0), axis=1, dtype=jnp.int32)) + row_ids
    flat_face = face_state.reshape(7, cell_total * SLOTS)
    return jnp.take(flat_face, source_row, axis=1)

def column_rates(extended, size_x):

    def one_column(column):
        strip = lax.dynamic_slice_in_dim(extended, column, 3, axis=1)
        return region_rates(strip)[:, 0]
    stacked = lax.map(one_column, jnp.arange(size_x, dtype=jnp.int32))
    return jnp.moveaxis(stacked, 0, 1)

def reference(particles, counts, leavers):
    size_x = particles.shape[1]
    fields = jnp.concatenate([particles, occupied(counts)[None]], axis=0)
    pad_plan = ((0, 0), (1, 1), (1, 1), (0, 0))
    rates_now = column_rates(jnp.pad(fields, pad_plan), size_x)
    midpoint = predict(fields, rates_now)
    updated = correct(fields, column_rates(jnp.pad(midpoint, pad_plan), size_x))
    grouped = counts.reshape(SLABS, CX, NY, CZ)
    grouped = grouped.at[:, 0].add(-leavers[0]).at[:, CX - 1].add(-leavers[1])
    kept = updated * occupied(grouped.reshape(NX, NY, CZ))[None]
    faces = updated.reshape(7, SLABS, CX, TILES, CY, CZ * SLOTS)
    face_counts = counts.reshape(SLABS, CX, TILES, CY, CZ)
    face_leave = leavers.reshape(2, SLABS, TILES, CY, CZ)
    packer = jax.vmap(jax.vmap(pack_leavers, in_axes=(1, 0, 0)), in_axes=(1, 0, 0))
    lower_rows = packer(faces[:, :, 0], face_counts[:, 0], face_leave[0])
    upper_rows = packer(faces[:, :, CX - 1], face_counts[:, CX - 1], face_leave[1])
    nothing = jnp.zeros_like(lower_rows[:1])
    from_below = jnp.concatenate([nothing, upper_rows[:-1]], axis=0)
    from_above = jnp.concatenate([lower_rows[1:], nothing], axis=0)
    arrivals = jnp.stack([from_below, from_above], axis=0)
    arrivals = jnp.transpose(arrivals, (0, 3, 1, 2, 4)).reshape(2, 7, SLABS * TILES * FACE_ROWS)
    return (kept, arrivals)
```

```python
import math

import jax
import jax.numpy as jnp
from jax import lax
from jax.experimental import pallas as pl
from jax.experimental.pallas import tpu as pltpu
from jax.sharding import PartitionSpec as P

SLOTS = 32
LMAX = 4
CZ = 48
BLOCKS = 12

sound_speed = 10.0
smoothing = 0.5
kernel_norm = 21.0 / (16.0 * math.pi * smoothing**3)
grad_scale = -5.0 * kernel_norm / (smoothing * smoothing)
eos_stiff = sound_speed * sound_speed / 7.0
particle_mass = 0.125
viscosity = 0.1
visc_floor = 0.01 * smoothing * smoothing
time_step = 0.01
gravity = 9.81
mass_grad = particle_mass * grad_scale
visc_gain = 2.0 * viscosity * sound_speed * smoothing
FAR = 1e15

OWN = [(0, 0), (0, 1), (1, 0), (1, 1)]


def column_rows(src, far_x, far_y, col, lhs):
    sub = lax.broadcasted_iota(jnp.int32, (8, 128), 0)
    shift = jnp.where(sub == 0, far_x, jnp.where(sub == 1, far_y, 0.0))
    high, mid, low = [], [], []
    for r in range(BLOCKS):
        vals = src[r]
        absent = jnp.broadcast_to(vals[6:7], (8, 128)) == 0.0
        vals = jnp.where((sub == 0) & absent, FAR, vals + shift)
        top = vals.astype(jnp.bfloat16).astype(jnp.float32)
        rest = vals - top
        second = rest.astype(jnp.bfloat16).astype(jnp.float32)
        high.append(top)
        mid.append(second)
        low.append(rest - second)
    pairs = [jnp.where(sub < 4, low[r], pltpu.roll(low[r + 6], 4, 0)) for r in range(6)]
    zero = jnp.zeros((8, 128), jnp.float32)
    first = jnp.concatenate(high + pairs[:4], axis=0)
    second = jnp.concatenate(mid + pairs[4:] + [zero, zero], axis=0)
    rows = pl.ds(pl.multiple_of(col * 128, 128), 128)
    lhs[rows, 0:128] = first.T.astype(jnp.bfloat16)
    lhs[rows, 128:256] = second.T.astype(jnp.bfloat16)


def select_matrix():
    k = lax.broadcasted_iota(jnp.int32, (256, 3072), 0)
    n = lax.broadcasted_iota(jnp.int32, (256, 3072), 1)
    local, sub = k % 128, k % 8
    whole = local < 96
    pair_row = (local - 96) // 8 + jnp.where(k < 128, 0, 4)
    field = jnp.where(whole, sub, sub % 4)
    row = jnp.where(whole, local // 8, pair_row + 6 * (sub // 4))
    row = jnp.where(k < 240, row, -1)
    want_field, beta, chunk = n // 384, (n // 128) % 3, (n % 128) // 32
    return ((field == want_field) & (row == 3 * chunk + beta)).astype(jnp.bfloat16)


def spread_columns(count, lhs, select, tiles, first):
    level = lax.broadcasted_iota(jnp.int32, (16, 8, 128), 0) // 4

    def two(n, _):
        rows = lhs[pl.ds(pl.multiple_of(n * 256, 256), 256), :]
        for t in range(12):
            out = jnp.dot(rows, select[:, 256 * t:256 * t + 256],
                          preferred_element_type=jnp.float32)
            for h in range(2):
                f, beta = (2 * t + h) // 3, (2 * t + h) % 3
                for m in range(2):
                    part = out[128 * m:128 * m + 128, 128 * h:128 * h + 128].reshape(16, 8, 128)
                    if f == 2:
                        part = part + (level + 4 * beta).astype(jnp.float32)
                    tiles[first + 2 * n + m, f, 16 * beta + 4:16 * beta + 20] = part
        return 0
    lax.fori_loop(0, count // 2, two, 0)
    chunk = lax.broadcasted_iota(jnp.int32, (8, 128), 1) // 32

    def edges(c, _):
        for s in range(4):
            for f in range(8):
                below = pltpu.roll(tiles[first + c, f, 48 + s], 32, 1)
                above = pltpu.roll(tiles[first + c, f, 4 + s], 96, 1)
                if f == 0:
                    below = jnp.where(chunk == 0, FAR, below)
                    above = jnp.where(chunk == 3, FAR, above)
                if f == 2:
                    below = below - 12.0
                    above = above + 12.0
                tiles[first + c, f, s] = below
                tiles[first + c, f, 52 + s] = above
        return 0
    lax.fori_loop(0, count, edges, 0)


def swap_chunks(load, store):
    chunk = lax.broadcasted_iota(jnp.int32, (8, 128), 1) // 32
    for beta in range(3):
        rows = [load(3 * g + beta) for g in range(4)]
        for q in range(4):
            res = rows[q]
            for g in range(4):
                if g != q:
                    res = jnp.where(chunk == g, pltpu.roll(rows[g], (32 * (g - q)) % 128, 1), res)
            store(4 * beta + q, res)


def swap_back(load, store):
    chunk = lax.broadcasted_iota(jnp.int32, (8, 128), 1) // 32
    for beta in range(3):
        rows = [load(4 * beta + q) for q in range(4)]
        for g in range(4):
            res = rows[g]
            for q in range(4):
                if g != q:
                    res = jnp.where(chunk == q, pltpu.roll(rows[q], (32 * (q - g)) % 128, 1), res)
            store(3 * g + beta, res)


def pair(acc, center, tile):
    xi, yi, zi, ui, vi, wi, di, ri = center
    dx = xi - tile[0]
    dy = yi - tile[1]
    dz = zi - tile[2]
    r2 = dx * dx + dy * dy + dz * dz
    approach = (tile[3] - ui) * dx + (tile[4] - vi) * dy + (tile[5] - wi) * dz
    dist = r2 * lax.rsqrt(jnp.maximum(r2, 1e-30))
    support = jnp.maximum(1.0 - dist, 0.0)
    slope = support * support * support
    visc = jnp.maximum(approach, 0.0) / ((r2 + visc_floor) * (di + tile[6]))
    force = (ri + tile[7] + visc) * slope
    return (acc[0] + force * dx, acc[1] + force * dy, acc[2] + force * dz,
            acc[3] + slope * approach)


def center_rows(rows, far_x, far_y, b):
    vals = [jnp.broadcast_to(rows[f:f + 1, :], (8, 128)) for f in range(8)]
    vals[0] = vals[0] + far_x
    vals[1] = vals[1] + far_y
    vals[2] = vals[2] + b.astype(jnp.float32)
    return vals


def center_blocks(own, blocks):
    def one(c, _):
        swap_chunks(lambda r: own[c, r], lambda r, v: blocks.__setitem__((c, r), v))
        return 0
    lax.fori_loop(0, 4, one, 0)


def all_pairs(blocks, tiles, neighbours, emit):
    def sums_at(c, cx, cy, b, js):
        center = center_rows(blocks[c, b], cx, cy, b)
        acc = tuple(jnp.zeros((8, 128), jnp.float32) for _ in range(4))
        for j in js:
            for d in range(3):
                for s in range(4):
                    acc = pair(acc, center, [tiles[j, f, (b + d) * 4 + s] for f in range(8)])
        emit(c, b, jnp.concatenate([jnp.sum(a, axis=0, keepdims=True) for a in acc]
                                   + [jnp.zeros((4, 128), jnp.float32)], axis=0))

    for c, (cx, cy) in enumerate(OWN):
        def step(b, _, c=c, cx=cx, cy=cy):
            sums_at(c, float(cx), float(cy), b, neighbours(cx, cy))
            return 0
        lax.fori_loop(0, BLOCKS, step, 0)


def near_kernel(own, select, acc_out, blocks, lhs, tiles):
    center_blocks(own, blocks)
    for c, (x, y) in enumerate(OWN):
        column_rows(own.at[c], float(x), float(y), c, lhs)
    spread_columns(4, lhs, select, tiles, 0)

    def emit(c, b, sums):
        acc_out[c, b] = sums
    all_pairs(blocks, tiles, lambda cx, cy: range(4), emit)


def slab_kernel(own, acc_in, low, high, select, acc_out, blocks, lhs, tiles):
    center_blocks(own, blocks)
    for n, (ref, x) in enumerate(((low, -1.0), (high, 2.0))):
        for y in range(2):
            column_rows(ref.at[y], x, float(y), 2 * n + y, lhs)
    spread_columns(4, lhs, select, tiles, 0)

    def emit(c, b, sums):
        acc_out[c, b] = sums + acc_in[c, b]
    all_pairs(blocks, tiles, lambda cx, cy: (2 * cx, 2 * cx + 1), emit)


def tile_kernel(final, base, own, acc_in, low, high, select, out, blocks, lhs, tiles, res):
    center_blocks(own, blocks)

    for n, (ref, y) in enumerate(((low, -1.0), (high, 2.0))):
        def one(i, _, n=n, ref=ref, y=y):
            column_rows(ref.at[i], (i - 1).astype(jnp.float32), y, 4 * n + i, lhs)
            return 0
        lax.fori_loop(0, 4, one, 0)
    spread_columns(8, lhs, select, tiles, 0)

    def emit(c, b, sums):
        res[c, b] = sums + acc_in[c, b]
    all_pairs(blocks, tiles, lambda cx, cy: range(4 * cy + cx, 4 * cy + cx + 3), emit)

    def finish(c, _):
        def store(r, rates):
            now = base[c, r]
            present = now[6:7] != 0.0
            ax = -mass_grad * rates[0:1]
            ay = -mass_grad * rates[1:2]
            az = -mass_grad * rates[2:3] - gravity
            drift = -mass_grad * rates[3:4]
            half = 0.5 * time_step
            if not final:
                dens = now[6:7] + half * drift
                dens = jnp.where(present, dens, 1.0)
                ratio = eos_stiff * (dens**7 - 1.0) / (dens * dens)
                vals = [now[0:1] + half * now[3:4], now[1:2] + half * now[4:5],
                        now[2:3] + half * now[5:6], now[3:4] + half * ax,
                        now[4:5] + half * ay, now[5:6] + half * az, dens, ratio]
            else:
                v1 = [now[3:4] + time_step * ax, now[4:5] + time_step * ay,
                      now[5:6] + time_step * az]
                vals = [now[k:k + 1] + half * (now[3 + k:4 + k] + v1[k]) for k in range(3)]
                vals += v1 + [now[6:7] + time_step * drift, now[7:8]]
            full = jnp.concatenate(vals, axis=0)
            out[c, r] = jnp.where(jnp.broadcast_to(present, (8, 128)), full, 0.0)
        swap_back(lambda r: res[c, r], store)
        return 0
    lax.fori_loop(0, 4, finish, 0)


def pair_call(body, name, columns, args, extra=()):
    return pl.pallas_call(
        body,
        out_shape=jax.ShapeDtypeStruct((4, BLOCKS, 8, 128), jnp.float32),
        scratch_shapes=[pltpu.VMEM((4, BLOCKS, 8, 128), jnp.float32),
                        pltpu.VMEM((columns * 128, 256), jnp.bfloat16),
                        pltpu.VMEM((columns, 8, 4 * BLOCKS + 8, 8, 128), jnp.float32),
                        *extra],
        compiler_params=pltpu.CompilerParams(vmem_limit_bytes=40 << 20),
        name=name,
    )(*args)


def rates_pass(final, base, own, select):
    low = shifted(own[2:4], "slab", 1)
    high = shifted(own[0:2], "slab", -1)
    acc = pair_call(near_kernel, "near_pairs", 4, (own, select))
    front = shifted(jnp.concatenate([low[1:2], own[1:2], own[3:4], high[1:2]]), "tile", 1)
    back = shifted(jnp.concatenate([low[0:1], own[0:1], own[2:3], high[0:1]]), "tile", -1)
    acc = pair_call(slab_kernel, "slab_pairs", 4, (own, acc, low, high, select))

    def body(*refs):
        tile_kernel(final, *refs)
    return pair_call(body, "tile_pairs_final" if final else "tile_pairs", 8,
                     (base, own, acc, front, back, select),
                     (pltpu.VMEM((4, BLOCKS, 8, 128), jnp.float32),))


def slot_mask(cell_counts):
    slot = lax.broadcasted_iota(jnp.int32, cell_counts.shape + (SLOTS,), cell_counts.ndim)
    return slot < cell_counts[..., None]


def pack_leavers(face_state, face_count, face_leave):
    cell_total = face_count.shape[0] * face_count.shape[1]
    row_total = cell_total * LMAX // 2
    leave_quota = face_leave.reshape(cell_total)
    occupancy = face_count.reshape(cell_total)
    row_ends = jnp.cumsum(leave_quota, dtype=jnp.int32)
    starts = row_ends - leave_quota
    row_ids = jnp.arange(row_total, dtype=jnp.int32)
    owner_mask = (starts[None, :] <= row_ids[:, None]) & (row_ends[None, :] > row_ids[:, None])
    root = jnp.arange(cell_total, dtype=jnp.int32) * SLOTS + occupancy - leave_quota - starts
    source_row = jnp.sum(jnp.where(owner_mask, root[None, :], 0), axis=1, dtype=jnp.int32) + row_ids
    flat_face = face_state.reshape(7, cell_total * SLOTS)
    return jnp.take(flat_face, source_row, axis=1)


def shifted(value, axis, steps):
    count = lax.axis_size(axis)
    leading, last = (max(0, -steps), min(count, count - steps))
    return lax.ppermute(value, axis, [(source, source + steps) for source in range(leading, last)])


def start_fields(particles, counts):
    mask = slot_mask(counts).reshape(2, 2, CZ * SLOTS)
    dens = jnp.where(mask, particles[6], 1.0)
    ratio = eos_stiff * (dens**7 - 1.0) / (dens * dens)
    fields = jnp.concatenate([particles, ratio[None]], axis=0)
    fields = jnp.where(mask[None], fields, 0.0)
    return fields.reshape(8, 4, BLOCKS, 128).transpose(1, 2, 0, 3)


def finish_fields(updated):
    return updated.transpose(2, 0, 1, 3)[:7].reshape(7, 2, 2, CZ * SLOTS)


def shards(particles, counts, leavers):
    fields = start_fields(particles, counts)
    select = select_matrix()
    middle = rates_pass(False, fields, fields, select)
    updated = finish_fields(rates_pass(True, fields, middle, select))
    remain = counts.at[0].add(-leavers[0, 0]).at[1].add(-leavers[1, 0])
    kept = jnp.where(slot_mask(remain).reshape(1, 2, 2, CZ * SLOTS), updated, 0.0)
    lower_rows = pack_leavers(updated[:, 0], counts[0], leavers[0, 0])
    upper_rows = pack_leavers(updated[:, 1], counts[1], leavers[1, 0])
    from_below = shifted(upper_rows, "slab", 1)
    from_above = shifted(lower_rows, "slab", -1)
    return (kept, jnp.stack([from_below, from_above], axis=0))


def solution(mesh):
    return jax.shard_map(
        shards,
        mesh=mesh,
        in_specs=(
            P(None, "slab", "tile", None),
            P("slab", "tile", None),
            P(None, "slab", "tile", None),
        ),
        out_specs=(P(None, "slab", "tile", None), P(None, None, ("slab", "tile"))),
        check_vma=False,
    )
```

```python
import math

import jax
import jax.numpy as jnp
from jax import lax
from jax.experimental import pallas as pl
from jax.experimental.pallas import tpu as pltpu
from jax.sharding import PartitionSpec as P

SLOTS = 32
LMAX = 4
CZ = 48
BLOCKS = 12

sound_speed = 10.0
smoothing = 0.5
kernel_norm = 21.0 / (16.0 * math.pi * smoothing**3)
grad_scale = -5.0 * kernel_norm / (smoothing * smoothing)
eos_stiff = sound_speed * sound_speed / 7.0
particle_mass = 0.125
viscosity = 0.1
visc_floor = 0.01 * smoothing * smoothing
time_step = 0.01
gravity = 9.81
mass_grad = particle_mass * grad_scale
visc_gain = 2.0 * viscosity * sound_speed * smoothing
FAR = 2.0**50
MIDDLE = 5.5
SPAN = 32 * (BLOCKS + 2)
AROUND = (0, 1, 2, 4, 5, 6, 8, 9, 10)


def pieces(vals):
    top = vals.astype(jnp.bfloat16).astype(jnp.float32)
    rest = vals - top
    second = rest.astype(jnp.bfloat16).astype(jnp.float32)
    return top, second, rest - second


def products(vals):
    both = []
    for prod in (vals * vals, vals * pltpu.roll(vals, 5, 0)):
        rows = [jnp.broadcast_to(prod[k:k + 1], (8, 128)) for k in range(3)]
        both.append(rows[0] + rows[1] + rows[2])
    return both


def neighbour_rows(vals, far_x, far_y, far_z, sub):
    absent = jnp.broadcast_to(vals[6:7], (8, 128)) == 0.0
    shift = jnp.where(sub == 0, far_x, jnp.where(sub == 1, far_y, jnp.where(sub == 2, far_z, 0.0)))
    vals = jnp.where(absent, jnp.where(sub == 0, FAR, 0.0), vals + shift)
    high, mid, low = pieces(vals)
    square, flow = products(vals)
    tail = jnp.ones((8, 128), jnp.float32)
    for k, part in enumerate(pieces(square) + pieces(flow)):
        tail = jnp.where(sub == k, part, tail)
    last = jnp.where(sub == 0, 1.0, 0.0)
    return [high, high, mid, high, low, mid, tail, last]


def column_features(src, far_x, far_y, col, lhs):
    sub = lax.broadcasted_iota(jnp.int32, (8, 128), 0)
    chunk = lax.broadcasted_iota(jnp.int32, (8, 128), 1) // 32
    for beta in range(4):
        rows = []
        for g in range(4):
            if beta < 3:
                vals = src[3 * g + beta]
                level = (chunk + 4 * beta).astype(jnp.float32)
            else:
                none = jnp.zeros((8, 128), jnp.float32)
                below = src[3 * g - 1] if g > 0 else none
                above = src[3 * g + 3] if g < 3 else none
                vals = jnp.where(chunk == 3, below, jnp.where(chunk == 0, above, 0.0))
                level = jnp.where(chunk == 3, -1.0, 12.0)
            rows += neighbour_rows(vals, far_x, far_y, level - MIDDLE, sub)
        for h in range(2):
            flat = jnp.concatenate(rows[16 * h:16 * h + 16], axis=0).T.astype(jnp.bfloat16)
            lanes = slice(128 * h, 128 * h + 128)
            if beta < 3:
                lhs[col, 128 * beta + 32:128 * beta + 160, lanes] = flat
            else:
                lhs[col, 0:32, lanes] = flat[96:128]
                lhs[col, 416:448, lanes] = flat[0:32]


def spread_positions(count, lhs, select, tiles):
    k = lax.broadcasted_iota(jnp.int32, (256, 384), 0)
    n = lax.broadcasted_iota(jnp.int32, (256, 384), 1)
    part = k % 64
    hit = (part % 8 == n // 128) & ((part // 8) % 2 == 0) & (part < 40) & (k // 64 == (n % 128) // 32)
    select[...] = jnp.where(hit, 1.0, 0.0).astype(jnp.bfloat16)

    def four(n, _):
        rows = lhs[pl.ds(4 * n, 4)].reshape(4 * SPAN, 256)
        out = jnp.dot(rows, select[...], preferred_element_type=jnp.float32)
        for c in range(4):
            for f in range(3):
                part = out[SPAN * c:SPAN * (c + 1), 128 * f:128 * f + 128]
                tiles[4 * n + c, f] = part.reshape(SPAN // 8, 8, 128)
        return 0
    lax.fori_loop(0, count // 4, four, 0)


def swap_chunks(load, store):
    chunk = lax.broadcasted_iota(jnp.int32, (8, 128), 1) // 32
    for beta in range(3):
        rows = [load(3 * g + beta) for g in range(4)]
        for q in range(4):
            res = rows[q]
            for g in range(4):
                if g != q:
                    res = jnp.where(chunk == g, pltpu.roll(rows[g], (32 * (g - q)) % 128, 1), res)
            store(4 * beta + q, res)


def swap_back(load, store):
    chunk = lax.broadcasted_iota(jnp.int32, (8, 128), 1) // 32
    for beta in range(3):
        rows = [load(4 * beta + q) for q in range(4)]
        for g in range(4):
            res = rows[g]
            for q in range(4):
                if g != q:
                    res = jnp.where(chunk == q, pltpu.roll(rows[q], (32 * (q - g)) % 128, 1), res)
            store(3 * g + beta, res)


def chunk_masks():
    chunk = lax.broadcasted_iota(jnp.int32, (16, 128), 1) // 32
    return [jnp.where(chunk == g, 1.0, 0.0).astype(jnp.bfloat16) for g in range(4)]


def fill_weights(weights):
    sub = lax.broadcasted_iota(jnp.int32, (8, 128), 0)
    zero = jnp.zeros((8, 128), jnp.float32)
    for n, k in ((2, 6), (3, 7)):
        one = jnp.where(sub == k, 1.0, 0.0)
        part = jnp.concatenate([one, zero], axis=0).astype(jnp.bfloat16)
        for g, mask in enumerate(chunk_masks()):
            for p in range(3):
                row = 64 * g + 16 * p
                weights[row:row + 16, 128 * n:128 * n + 128] = part * mask


def center_weights(rows, weights):
    sub = lax.broadcasted_iota(jnp.int32, (8, 128), 0)
    parts = pieces(rows)
    square, flow = products(rows)
    place = [jnp.where(sub < 3, -2.0 * p, 0.0) for p in parts]
    speed = [jnp.where(sub < 3, pltpu.roll(p, 5, 0), jnp.where(sub < 6, pltpu.roll(p, 3, 0), 0.0))
             for p in parts]

    def tail(lead, const):
        top, second, third = const
        return [jnp.where(sub == 6, top, jnp.where(sub == 7, second, lead)),
                jnp.where(sub == 0, third, 0.0)]

    def over(k):
        return [jnp.broadcast_to(p[k:k + 1], (8, 128)) for p in parts]
    masks = chunk_masks()
    tails = [tail(jnp.where(sub < 3, 1.0, 0.0), pieces(square)),
             tail(jnp.where((sub >= 3) & (sub < 6), -1.0, 0.0), pieces(-flow)),
             tail(jnp.zeros((8, 128), jnp.float32), over(6)),
             tail(jnp.zeros((8, 128), jnp.float32), over(7))]
    for n, last in enumerate(tails):
        blocks = [(3, last)]
        if n < 2:
            p = (place, speed)[n]
            blocks += [(0, p[:2]), (1, [p[0], p[2]]), (2, p[:2])]
        for at, part in blocks:
            part = jnp.concatenate(part, axis=0).astype(jnp.bfloat16)
            for g, mask in enumerate(masks):
                row = 64 * g + 16 * at
                weights[row:row + 16, 128 * n:128 * n + 128] = part * mask


def pair(acc, terms, tile):
    r2, approach, dens, ratio = terms
    r2 = jnp.maximum(r2, 1e-30)
    support = jnp.maximum(1.0 - r2 * lax.rsqrt(r2), 0.0)
    slope = support * support * support
    visc = jnp.maximum(approach, 0.0) / ((r2 + visc_floor) * dens)
    force = (ratio + visc) * slope
    return (acc[0] + force * tile[0], acc[1] + force * tile[1], acc[2] + force * tile[2],
            acc[3] + slope * approach, acc[4] + force)


def center_blocks(own, blocks):
    sub = lax.broadcasted_iota(jnp.int32, (8, 128), 0)

    def one(c, _):
        far_x = (c // 2).astype(jnp.float32) - 0.5
        far_y = (c % 2).astype(jnp.float32) - 0.5

        def store(r, vals):
            shift = jnp.where(sub == 0, far_x, jnp.where(sub == 1, far_y,
                              jnp.where(sub == 2, r - MIDDLE, 0.0)))
            blocks[c, r] = vals + shift
        swap_chunks(lambda r: own[c, r], store)
        return 0
    lax.fori_loop(0, 4, one, 0)


def all_pairs(blocks, lhs, tiles, bufs, emit):
    def first_column(c):
        return 4 * (c // 2) + c % 2

    def produce(n, weights, result):
        n = jnp.minimum(n, 4 * BLOCKS - 1)
        c, b = n // BLOCKS, n % BLOCKS
        center_weights(blocks[c, b], weights)
        rows = pl.ds(pl.multiple_of(32 * b, 32), 96)
        near = jnp.concatenate([lhs[first_column(c) + j, rows, :] for j in AROUND], axis=0)
        result[...] = jnp.dot(near, weights[...], preferred_element_type=jnp.float32)

    def consume(n, result):
        c, b = n // BLOCKS, n % BLOCKS
        acc = tuple(jnp.zeros((8, 128), jnp.float32) for _ in range(5))
        for k, j in enumerate(AROUND):
            for i in range(12):
                r = 96 * k + 8 * i
                terms = [result[r:r + 8, 128 * n:128 * n + 128] for n in range(4)]
                acc = pair(acc, terms, [tiles[first_column(c) + j, f, 4 * b + i] for f in range(3)])
        sums = [jnp.sum(a, axis=0, keepdims=True) for a in acc]
        rows = blocks[c, b]
        sums = [rows[k:k + 1] * sums[4] - sums[k] for k in range(3)] + sums[3:4]
        emit(c, b, jnp.concatenate(sums + [jnp.zeros((4, 128), jnp.float32)], axis=0))

    w0, r0, w1, r1 = bufs
    fill_weights(w0)
    fill_weights(w1)
    produce(0, w0, r0)

    def step(m, _):
        produce(2 * m + 1, w1, r1)
        consume(2 * m, r0)
        produce(2 * m + 2, w0, r0)
        consume(2 * m + 1, r1)
        return 0
    lax.fori_loop(0, 2 * BLOCKS, step, 0)


def pass_kernel(final, base, own, low, high, front, back, out,
                cols, blocks, lhs, tiles, select, res, *bufs):
    center_blocks(own, blocks)
    for i in range(2):
        for y in range(2):
            cols[4 * (i + 1) + y + 1] = own[2 * i + y]
        cols[1 + i] = low[i]
        cols[13 + i] = high[i]
    for i in range(4):
        cols[4 * i] = front[i]
        cols[4 * i + 3] = back[i]

    def one(j, _):
        column_features(cols.at[j], (j // 4).astype(jnp.float32) - 1.5,
                        (j % 4).astype(jnp.float32) - 1.5, j, lhs)
        return 0
    lax.fori_loop(0, 16, one, 0)
    spread_positions(16, lhs, select, tiles)

    def emit(c, b, sums):
        res[c, b] = sums
    all_pairs(blocks, lhs, tiles, bufs, emit)

    def finish(c, _):
        def store(r, rates):
            now = base[c, r]
            present = now[6:7] != 0.0
            ax = -mass_grad * rates[0:1]
            ay = -mass_grad * rates[1:2]
            az = -mass_grad * rates[2:3] - gravity
            drift = -mass_grad * rates[3:4]
            half = 0.5 * time_step
            if not final:
                dens = now[6:7] + half * drift
                dens = jnp.where(present, dens, 1.0)
                ratio = eos_stiff * (dens**7 - 1.0) / (dens * dens)
                vals = [now[0:1] + half * now[3:4], now[1:2] + half * now[4:5],
                        now[2:3] + half * now[5:6], now[3:4] + half * ax,
                        now[4:5] + half * ay, now[5:6] + half * az, dens, ratio]
            else:
                v1 = [now[3:4] + time_step * ax, now[4:5] + time_step * ay,
                      now[5:6] + time_step * az]
                vals = [now[k:k + 1] + half * (now[3 + k:4 + k] + v1[k]) for k in range(3)]
                vals += v1 + [now[6:7] + time_step * drift, now[7:8]]
            full = jnp.concatenate(vals, axis=0)
            out[c, r] = jnp.where(jnp.broadcast_to(present, (8, 128)), full, 0.0)
        swap_back(lambda r: res[c, r], store)
        return 0
    lax.fori_loop(0, 4, finish, 0)


def rates_pass(final, base, own):
    low = shifted(own[2:4], "slab", 1)
    high = shifted(own[0:2], "slab", -1)
    front = shifted(jnp.concatenate([low[1:2], own[1:2], own[3:4], high[1:2]]), "tile", 1)
    back = shifted(jnp.concatenate([low[0:1], own[0:1], own[2:3], high[0:1]]), "tile", -1)

    def body(*refs):
        pass_kernel(final, *refs)
    work = [pltpu.VMEM((256, 512), jnp.bfloat16), pltpu.VMEM((864, 512), jnp.float32)]
    return pl.pallas_call(
        body,
        out_shape=jax.ShapeDtypeStruct((4, BLOCKS, 8, 128), jnp.float32),
        scratch_shapes=[pltpu.VMEM((16, BLOCKS, 8, 128), jnp.float32),
                        pltpu.VMEM((4, BLOCKS, 8, 128), jnp.float32),
                        pltpu.VMEM((16, SPAN, 256), jnp.bfloat16),
                        pltpu.VMEM((16, 3, SPAN // 8, 8, 128), jnp.float32),
                        pltpu.VMEM((256, 384), jnp.bfloat16),
                        pltpu.VMEM((4, BLOCKS, 8, 128), jnp.float32),
                        *work, *work],
        compiler_params=pltpu.CompilerParams(vmem_limit_bytes=40 << 20),
        name="correct_pass" if final else "predict_pass",
    )(base, own, low, high, front, back)


def slot_mask(cell_counts):
    slot = lax.broadcasted_iota(jnp.int32, cell_counts.shape + (SLOTS,), cell_counts.ndim)
    return slot < cell_counts[..., None]


def pack_leavers(face_state, face_count, face_leave):
    cell_total = face_count.shape[0] * face_count.shape[1]
    row_total = cell_total * LMAX // 2
    leave_quota = face_leave.reshape(cell_total)
    occupancy = face_count.reshape(cell_total)
    row_ends = jnp.cumsum(leave_quota, dtype=jnp.int32)
    starts = row_ends - leave_quota
    row_ids = jnp.arange(row_total, dtype=jnp.int32)
    owner_mask = (starts[None, :] <= row_ids[:, None]) & (row_ends[None, :] > row_ids[:, None])
    root = jnp.arange(cell_total, dtype=jnp.int32) * SLOTS + occupancy - leave_quota - starts
    source_row = jnp.sum(jnp.where(owner_mask, root[None, :], 0), axis=1, dtype=jnp.int32) + row_ids
    flat_face = face_state.reshape(7, cell_total * SLOTS)
    return jnp.take(flat_face, source_row, axis=1)


def shifted(value, axis, steps):
    count = lax.axis_size(axis)
    leading, last = (max(0, -steps), min(count, count - steps))
    return lax.ppermute(value, axis, [(source, source + steps) for source in range(leading, last)])


def start_fields(particles, counts):
    mask = slot_mask(counts).reshape(2, 2, CZ * SLOTS)
    dens = jnp.where(mask, particles[6], 1.0)
    ratio = eos_stiff * (dens**7 - 1.0) / (dens * dens)
    fields = jnp.concatenate([particles, ratio[None]], axis=0)
    fields = jnp.where(mask[None], fields, 0.0)
    return fields.reshape(8, 4, BLOCKS, 128).transpose(1, 2, 0, 3)


def finish_fields(updated):
    return updated.transpose(2, 0, 1, 3)[:7].reshape(7, 2, 2, CZ * SLOTS)


def shards(particles, counts, leavers):
    fields = start_fields(particles, counts)
    middle = rates_pass(False, fields, fields)
    updated = finish_fields(rates_pass(True, fields, middle))
    remain = counts.at[0].add(-leavers[0, 0]).at[1].add(-leavers[1, 0])
    kept = jnp.where(slot_mask(remain).reshape(1, 2, 2, CZ * SLOTS), updated, 0.0)
    lower_rows = pack_leavers(updated[:, 0], counts[0], leavers[0, 0])
    upper_rows = pack_leavers(updated[:, 1], counts[1], leavers[1, 0])
    from_below = shifted(upper_rows, "slab", 1)
    from_above = shifted(lower_rows, "slab", -1)
    return (kept, jnp.stack([from_below, from_above], axis=0))


def solution(mesh):
    return jax.shard_map(
        shards,
        mesh=mesh,
        in_specs=(
            P(None, "slab", "tile", None),
            P("slab", "tile", None),
            P(None, "slab", "tile", None),
        ),
        out_specs=(P(None, "slab", "tile", None), P(None, None, ("slab", "tile"))),
        check_vma=False,
    )
```

```python
import math

import jax
import jax.numpy as jnp
from jax import lax
from jax.experimental import pallas as pl
from jax.experimental.pallas import tpu as pltpu
from jax.sharding import PartitionSpec as P

SLOTS = 32
LMAX = 4
CZ = 48
BLOCKS = 12

sound_speed = 10.0
smoothing = 0.5
kernel_norm = 21.0 / (16.0 * math.pi * smoothing**3)
grad_scale = -5.0 * kernel_norm / (smoothing * smoothing)
eos_stiff = sound_speed * sound_speed / 7.0
particle_mass = 0.125
viscosity = 0.1
visc_floor = 0.01 * smoothing * smoothing
time_step = 0.01
gravity = 9.81
mass_grad = particle_mass * grad_scale
visc_gain = 2.0 * viscosity * sound_speed * smoothing
FAR = 2.0**50
MIDDLE = 5.5
SPAN = 32 * (BLOCKS + 2)
AROUND = (0, 1, 2, 4, 5, 6, 8, 9, 10)


def pieces(vals):
    top = vals.astype(jnp.bfloat16).astype(jnp.float32)
    rest = vals - top
    second = rest.astype(jnp.bfloat16).astype(jnp.float32)
    return top, second, rest - second


def products(vals):
    both = []
    for prod in (vals * vals, vals * pltpu.roll(vals, 5, 0)):
        rows = [jnp.broadcast_to(prod[k:k + 1], (8, 128)) for k in range(3)]
        both.append(rows[0] + rows[1] + rows[2])
    return both


def neighbour_rows(vals, far_x, far_y, far_z, sub):
    absent = jnp.broadcast_to(vals[6:7], (8, 128)) == 0.0
    shift = jnp.where(sub == 0, far_x, jnp.where(sub == 1, far_y, jnp.where(sub == 2, far_z, 0.0)))
    vals = jnp.where(absent, jnp.where(sub == 0, FAR, 0.0), vals + shift)
    high, mid, low = pieces(vals)
    square, flow = products(vals)
    tail = jnp.ones((8, 128), jnp.float32)
    for k, part in enumerate(pieces(square) + pieces(flow)):
        tail = jnp.where(sub == k, part, tail)
    last = jnp.where(sub == 0, 1.0, 0.0)
    return [high, high, mid, high, low, mid, tail, last]


def column_features(src, far_x, far_y, col, lhs):
    sub = lax.broadcasted_iota(jnp.int32, (8, 128), 0)
    chunk = lax.broadcasted_iota(jnp.int32, (8, 128), 1) // 32
    for beta in range(4):
        rows = []
        for g in range(4):
            if beta < 3:
                vals = src[3 * g + beta]
                level = (chunk + 4 * beta).astype(jnp.float32)
            else:
                none = jnp.zeros((8, 128), jnp.float32)
                below = src[3 * g - 1] if g > 0 else none
                above = src[3 * g + 3] if g < 3 else none
                vals = jnp.where(chunk == 3, below, jnp.where(chunk == 0, above, 0.0))
                level = jnp.where(chunk == 3, -1.0, 12.0)
            rows += neighbour_rows(vals, far_x, far_y, level - MIDDLE, sub)
        for h in range(2):
            flat = jnp.concatenate(rows[16 * h:16 * h + 16], axis=0).T.astype(jnp.bfloat16)
            lanes = slice(128 * h, 128 * h + 128)
            if beta < 3:
                lhs[col, 128 * beta + 32:128 * beta + 160, lanes] = flat
            else:
                lhs[col, 0:32, lanes] = flat[96:128]
                lhs[col, 416:448, lanes] = flat[0:32]


def spread_positions(count, lhs, select, tiles):
    k = lax.broadcasted_iota(jnp.int32, (256, 384), 0)
    n = lax.broadcasted_iota(jnp.int32, (256, 384), 1)
    part = k % 64
    hit = (part % 8 == n // 128) & ((part // 8) % 2 == 0) & (part < 40) & (k // 64 == (n % 128) // 32)
    select[...] = jnp.where(hit, 1.0, 0.0).astype(jnp.bfloat16)

    def four(n, _):
        rows = lhs[pl.ds(4 * n, 4)].reshape(4 * SPAN, 256)
        out = jnp.dot(rows, select[...], preferred_element_type=jnp.float32)
        for c in range(4):
            for f in range(3):
                part = out[SPAN * c:SPAN * (c + 1), 128 * f:128 * f + 128]
                tiles[4 * n + c, f] = part.reshape(SPAN // 8, 8, 128)
        return 0
    lax.fori_loop(0, count // 4, four, 0)


def swap_chunks(load, store):
    chunk = lax.broadcasted_iota(jnp.int32, (8, 128), 1) // 32
    for beta in range(3):
        rows = [load(3 * g + beta) for g in range(4)]
        for q in range(4):
            res = rows[q]
            for g in range(4):
                if g != q:
                    res = jnp.where(chunk == g, pltpu.roll(rows[g], (32 * (g - q)) % 128, 1), res)
            store(4 * beta + q, res)


def swap_back(load, store):
    chunk = lax.broadcasted_iota(jnp.int32, (8, 128), 1) // 32
    for beta in range(3):
        rows = [load(4 * beta + q) for q in range(4)]
        for g in range(4):
            res = rows[g]
            for q in range(4):
                if g != q:
                    res = jnp.where(chunk == q, pltpu.roll(rows[q], (32 * (q - g)) % 128, 1), res)
            store(3 * g + beta, res)


def chunk_masks():
    chunk = lax.broadcasted_iota(jnp.int32, (16, 128), 1) // 32
    return [jnp.where(chunk == g, 1.0, 0.0).astype(jnp.bfloat16) for g in range(4)]


def fill_weights(weights):
    sub = lax.broadcasted_iota(jnp.int32, (8, 128), 0)
    zero = jnp.zeros((8, 128), jnp.float32)
    for n, k in ((2, 6), (3, 7)):
        one = jnp.where(sub == k, 1.0, 0.0)
        part = jnp.concatenate([one, zero], axis=0).astype(jnp.bfloat16)
        for g, mask in enumerate(chunk_masks()):
            for p in range(3):
                row = 64 * g + 16 * p
                weights[row:row + 16, 128 * n:128 * n + 128] = part * mask


def center_weights(rows, weights):
    sub = lax.broadcasted_iota(jnp.int32, (8, 128), 0)
    parts = pieces(rows)
    square, flow = products(rows)
    place = [jnp.where(sub < 3, -2.0 * p, 0.0) for p in parts]
    speed = [jnp.where(sub < 3, pltpu.roll(p, 5, 0), jnp.where(sub < 6, pltpu.roll(p, 3, 0), 0.0))
             for p in parts]

    def tail(lead, const):
        top, second, third = const
        return [jnp.where(sub == 6, top, jnp.where(sub == 7, second, lead)),
                jnp.where(sub == 0, third, 0.0)]

    def over(k):
        return [jnp.broadcast_to(p[k:k + 1], (8, 128)) for p in parts]
    masks = chunk_masks()
    tails = [tail(jnp.where(sub < 3, 1.0, 0.0), pieces(square)),
             tail(jnp.where((sub >= 3) & (sub < 6), -1.0, 0.0), pieces(-flow)),
             tail(jnp.zeros((8, 128), jnp.float32), over(6)),
             tail(jnp.zeros((8, 128), jnp.float32), over(7))]
    for n, last in enumerate(tails):
        blocks = [(3, last)]
        if n < 2:
            p = (place, speed)[n]
            blocks += [(0, p[:2]), (1, [p[0], p[2]]), (2, p[:2])]
        for at, part in blocks:
            part = jnp.concatenate(part, axis=0).astype(jnp.bfloat16)
            for g, mask in enumerate(masks):
                row = 64 * g + 16 * at
                weights[row:row + 16, 128 * n:128 * n + 128] = part * mask


def pair(acc, terms, tile):
    r2, approach, dens, ratio = terms
    r2 = jnp.maximum(r2, 1e-30)
    support = jnp.maximum(1.0 - r2 * lax.rsqrt(r2), 0.0)
    slope = support * support * support
    visc = jnp.maximum(approach, 0.0) / ((r2 + visc_floor) * dens)
    force = (ratio + visc) * slope
    return (acc[0] + force * tile[0], acc[1] + force * tile[1], acc[2] + force * tile[2],
            acc[3] + slope * approach, acc[4] + force)


def center_blocks(own, blocks):
    sub = lax.broadcasted_iota(jnp.int32, (8, 128), 0)

    def one(c, _):
        far_x = (c // 2).astype(jnp.float32) - 0.5
        far_y = (c % 2).astype(jnp.float32) - 0.5

        def store(r, vals):
            shift = jnp.where(sub == 0, far_x, jnp.where(sub == 1, far_y,
                              jnp.where(sub == 2, r - MIDDLE, 0.0)))
            blocks[c, r] = vals + shift
        swap_chunks(lambda r: own[c, r], store)
        return 0
    lax.fori_loop(0, 4, one, 0)


def all_pairs(blocks, lhs, tiles, bufs, emit):
    def first_column(c):
        return 4 * (c // 2) + c % 2

    def produce(n, weights, result):
        n = jnp.minimum(n, 4 * BLOCKS - 1)
        c, b = n // BLOCKS, n % BLOCKS
        center_weights(blocks[c, b], weights)
        rows = pl.ds(pl.multiple_of(32 * b, 32), 96)
        near = jnp.concatenate([lhs[first_column(c) + j, rows, :] for j in AROUND], axis=0)
        result[...] = jnp.dot(near, weights[...], preferred_element_type=jnp.float32)

    def consume(n, result):
        c, b = n // BLOCKS, n % BLOCKS
        acc = tuple(jnp.zeros((8, 128), jnp.float32) for _ in range(5))
        for k, j in enumerate(AROUND):
            for i in range(12):
                r = 96 * k + 8 * i
                terms = [result[r:r + 8, 128 * n:128 * n + 128] for n in range(4)]
                acc = pair(acc, terms, [tiles[first_column(c) + j, f, 4 * b + i] for f in range(3)])
        sums = [jnp.sum(a, axis=0, keepdims=True) for a in acc]
        rows = blocks[c, b]
        sums = [rows[k:k + 1] * sums[4] - sums[k] for k in range(3)] + sums[3:4]
        emit(c, b, jnp.concatenate(sums + [jnp.zeros((4, 128), jnp.float32)], axis=0))

    fill_weights(bufs[0])
    fill_weights(bufs[2])
    produce(0, *bufs[:2])

    def step(m, _):
        for k in range(4):
            consume(4 * m + k, bufs[2 * (k % 2) + 1])
            produce(4 * m + k + 1, *bufs[2 * ((k + 1) % 2):2 * ((k + 1) % 2) + 2])
        return 0
    lax.fori_loop(0, BLOCKS, step, 0)


def pass_kernel(final, base, own, slab_a, slab_b, tile_a, tile_b, out,
                cols, blocks, lhs, tiles, select, res, *bufs):
    center_blocks(own, blocks)
    odd_s = lax.axis_index("slab") % 2
    odd_t = lax.axis_index("tile") % 2
    x_a, y_a = 3 - 3 * odd_s, 3 - 3 * odd_t
    x_b, y_b = 3 - x_a, 3 - y_a
    for i in range(2):
        for y in range(2):
            cols[4 * (i + 1) + y + 1] = own[2 * i + y]
        cols[4 * x_a + 1 + i] = slab_a[i]
        cols[4 * x_b + 1 + i] = slab_b[i]
    for ref, y in ((tile_a, y_a), (tile_b, y_b)):
        cols[4 * x_a + y] = ref[0]
        cols[4 + y] = ref[1]
        cols[8 + y] = ref[2]
        cols[4 * x_b + y] = ref[3]

    def one(j, _):
        column_features(cols.at[j], (j // 4).astype(jnp.float32) - 1.5,
                        (j % 4).astype(jnp.float32) - 1.5, j, lhs)
        return 0
    lax.fori_loop(0, 16, one, 0)
    spread_positions(16, lhs, select, tiles)

    def emit(c, b, sums):
        res[c, b] = sums
    all_pairs(blocks, lhs, tiles, bufs, emit)

    def finish(c, _):
        def store(r, rates):
            now = base[c, r]
            present = now[6:7] != 0.0
            ax = -mass_grad * rates[0:1]
            ay = -mass_grad * rates[1:2]
            az = -mass_grad * rates[2:3] - gravity
            drift = -mass_grad * rates[3:4]
            half = 0.5 * time_step
            if not final:
                dens = now[6:7] + half * drift
                dens = jnp.where(present, dens, 1.0)
                ratio = eos_stiff * (dens**7 - 1.0) / (dens * dens)
                vals = [now[0:1] + half * now[3:4], now[1:2] + half * now[4:5],
                        now[2:3] + half * now[5:6], now[3:4] + half * ax,
                        now[4:5] + half * ay, now[5:6] + half * az, dens, ratio]
            else:
                v1 = [now[3:4] + time_step * ax, now[4:5] + time_step * ay,
                      now[5:6] + time_step * az]
                vals = [now[k:k + 1] + half * (now[3 + k:4 + k] + v1[k]) for k in range(3)]
                vals += v1 + [now[6:7] + time_step * drift, now[7:8]]
            full = jnp.concatenate(vals, axis=0)
            out[c, r] = jnp.where(jnp.broadcast_to(present, (8, 128)), full, 0.0)
        swap_back(lambda r: res[c, r], store)
        return 0
    lax.fori_loop(0, 4, finish, 0)


def swapped(value, axis, first):
    count = lax.axis_size(axis)
    trades = []
    for i in range(first, count - 1, 2):
        trades += [(i, i + 1), (i + 1, i)]
    return lax.ppermute(value, axis, trades)


def rates_pass(final, base, own):
    odd_s = lax.axis_index("slab") % 2
    odd_t = lax.axis_index("tile") % 2
    grid = own.reshape(2, 2, BLOCKS, 8, 128)
    slabs = [swapped(lax.dynamic_index_in_dim(grid, (1 - odd_s + k) % 2, 0, False), "slab", k)
             for k in range(2)]

    def edge(k):
        at = (1 - odd_t + k) % 2
        four = jnp.stack([slabs[0], grid[0], grid[1], slabs[1]])
        return lax.dynamic_index_in_dim(four, at, 1, False)
    tiles = [swapped(edge(k), "tile", k) for k in range(2)]

    def body(*refs):
        pass_kernel(final, *refs)
    work = [pltpu.VMEM((256, 512), jnp.bfloat16), pltpu.VMEM((864, 512), jnp.float32)]
    return pl.pallas_call(
        body,
        out_shape=jax.ShapeDtypeStruct((4, BLOCKS, 8, 128), jnp.float32),
        scratch_shapes=[pltpu.VMEM((16, BLOCKS, 8, 128), jnp.float32),
                        pltpu.VMEM((4, BLOCKS, 8, 128), jnp.float32),
                        pltpu.VMEM((16, SPAN, 256), jnp.bfloat16),
                        pltpu.VMEM((16, 3, SPAN // 8, 8, 128), jnp.float32),
                        pltpu.VMEM((256, 384), jnp.bfloat16),
                        pltpu.VMEM((4, BLOCKS, 8, 128), jnp.float32),
                        *work, *work],
        compiler_params=pltpu.CompilerParams(vmem_limit_bytes=40 << 20),
        name="correct_pass" if final else "predict_pass",
    )(base, own, *slabs, *tiles)


def slot_mask(cell_counts):
    slot = lax.broadcasted_iota(jnp.int32, cell_counts.shape + (SLOTS,), cell_counts.ndim)
    return slot < cell_counts[..., None]


def pack_leavers(face_state, face_count, face_leave):
    cell_total = face_count.shape[0] * face_count.shape[1]
    row_total = cell_total * LMAX // 2
    leave_quota = face_leave.reshape(cell_total)
    occupancy = face_count.reshape(cell_total)
    row_ends = jnp.cumsum(leave_quota, dtype=jnp.int32)
    starts = row_ends - leave_quota
    row_ids = jnp.arange(row_total, dtype=jnp.int32)
    owner_mask = (starts[None, :] <= row_ids[:, None]) & (row_ends[None, :] > row_ids[:, None])
    root = jnp.arange(cell_total, dtype=jnp.int32) * SLOTS + occupancy - leave_quota - starts
    source_row = jnp.sum(jnp.where(owner_mask, root[None, :], 0), axis=1, dtype=jnp.int32) + row_ids
    flat_face = face_state.reshape(7, cell_total * SLOTS)
    return jnp.take(flat_face, source_row, axis=1)


def start_fields(particles, counts):
    mask = slot_mask(counts).reshape(2, 2, CZ * SLOTS)
    dens = jnp.where(mask, particles[6], 1.0)
    ratio = eos_stiff * (dens**7 - 1.0) / (dens * dens)
    fields = jnp.concatenate([particles, ratio[None]], axis=0)
    fields = jnp.where(mask[None], fields, 0.0)
    return fields.reshape(8, 4, BLOCKS, 128).transpose(1, 2, 0, 3)


def finish_fields(updated):
    return updated.transpose(2, 0, 1, 3)[:7].reshape(7, 2, 2, CZ * SLOTS)


def shards(particles, counts, leavers):
    fields = start_fields(particles, counts)
    middle = rates_pass(False, fields, fields)
    updated = finish_fields(rates_pass(True, fields, middle))
    remain = counts.at[0].add(-leavers[0, 0]).at[1].add(-leavers[1, 0])
    kept = jnp.where(slot_mask(remain).reshape(1, 2, 2, CZ * SLOTS), updated, 0.0)
    lower_rows = pack_leavers(updated[:, 0], counts[0], leavers[0, 0])
    upper_rows = pack_leavers(updated[:, 1], counts[1], leavers[1, 0])
    odd = lax.axis_index("slab") % 2 == 1
    first = swapped(jnp.where(odd, lower_rows, upper_rows), "slab", 0)
    second = swapped(jnp.where(odd, upper_rows, lower_rows), "slab", 1)
    return (kept, jnp.stack([jnp.where(odd, first, second), jnp.where(odd, second, first)]))


def solution(mesh):
    return jax.shard_map(
        shards,
        mesh=mesh,
        in_specs=(
            P(None, "slab", "tile", None),
            P("slab", "tile", None),
            P(None, "slab", "tile", None),
        ),
        out_specs=(P(None, "slab", "tile", None), P(None, None, ("slab", "tile"))),
        check_vma=False,
    )
```

```python
import math

import jax
import jax.numpy as jnp
from jax import lax
from jax.experimental import pallas as pl
from jax.experimental.pallas import tpu as pltpu
from jax.sharding import PartitionSpec as P

SLOTS = 32
LMAX = 4
CZ = 48
BLOCKS = 12

sound_speed = 10.0
smoothing = 0.5
kernel_norm = 21.0 / (16.0 * math.pi * smoothing**3)
grad_scale = -5.0 * kernel_norm / (smoothing * smoothing)
eos_stiff = sound_speed * sound_speed / 7.0
particle_mass = 0.125
viscosity = 0.1
visc_floor = 0.01 * smoothing * smoothing
time_step = 0.01
gravity = 9.81
mass_grad = particle_mass * grad_scale
visc_gain = 2.0 * viscosity * sound_speed * smoothing
FAR = 2.0**50
MIDDLE = 5.5
UNROLL = 12
SPAN = 32 * (BLOCKS + 2)
AROUND = (0, 1, 2, 4, 5, 6, 8, 9, 10)


def pieces(vals):
    top = vals.astype(jnp.bfloat16).astype(jnp.float32)
    rest = vals - top
    second = rest.astype(jnp.bfloat16).astype(jnp.float32)
    return top, second, rest - second


def products(vals):
    both = []
    for prod in (vals * vals, vals * pltpu.roll(vals, 5, 0)):
        rows = [jnp.broadcast_to(prod[k:k + 1], (8, 128)) for k in range(3)]
        both.append(rows[0] + rows[1] + rows[2])
    return both


def neighbour_rows(vals, far_x, far_y, far_z, sub):
    absent = jnp.broadcast_to(vals[6:7], (8, 128)) == 0.0
    shift = jnp.where(sub == 0, far_x, jnp.where(sub == 1, far_y, jnp.where(sub == 2, far_z, 0.0)))
    vals = jnp.where(absent, jnp.where(sub == 0, FAR, 0.0), vals + shift)
    high, mid, low = pieces(vals)
    square, flow = products(vals)
    tail = jnp.ones((8, 128), jnp.float32)
    for k, part in enumerate(pieces(square) + pieces(flow)):
        tail = jnp.where(sub == k, part, tail)
    last = jnp.where(sub == 0, 1.0, 0.0)
    turned = pltpu.roll(low, 6, 0)
    places = [jnp.where(sub < 3, high, jnp.where(sub < 6, pltpu.roll(mid, 3, 0), turned)),
              jnp.where(sub == 0, turned, jnp.where(sub == 1, 1.0, 0.0))]
    return [high, high, mid, high, low, mid, tail, last], places


def column_features(src, far_x, far_y, col, lhs, places):
    sub = lax.broadcasted_iota(jnp.int32, (8, 128), 0)
    chunk = lax.broadcasted_iota(jnp.int32, (8, 128), 1) // 32
    for beta in range(4):
        rows = []
        for g in range(4):
            if beta < 3:
                vals = src[3 * g + beta]
                level = (chunk + 4 * beta).astype(jnp.float32)
            else:
                none = jnp.zeros((8, 128), jnp.float32)
                below = src[3 * g - 1] if g > 0 else none
                above = src[3 * g + 3] if g < 3 else none
                vals = jnp.where(chunk == 3, below, jnp.where(chunk == 0, above, 0.0))
                level = jnp.where(chunk == 3, -1.0, 12.0)
            more, put = neighbour_rows(vals, far_x, far_y, level - MIDDLE, sub)
            rows += more
            put = jnp.concatenate(put, axis=0).astype(jnp.bfloat16)
            for tile in ((beta + 1,) if beta < 3 else (0, 4)):
                places[col, tile, 16 * g:16 * g + 16] = put
        for h in range(2):
            flat = jnp.concatenate(rows[16 * h:16 * h + 16], axis=0).T.astype(jnp.bfloat16)
            lanes = slice(128 * h, 128 * h + 128)
            if beta < 3:
                lhs[col, 128 * beta + 32:128 * beta + 160, lanes] = flat
            else:
                lhs[col, 0:32, lanes] = flat[96:128]
                lhs[col, 416:448, lanes] = flat[0:32]


def swap_chunks(load, store):
    chunk = lax.broadcasted_iota(jnp.int32, (8, 128), 1) // 32
    for beta in range(3):
        rows = [load(3 * g + beta) for g in range(4)]
        for q in range(4):
            res = rows[q]
            for g in range(4):
                if g != q:
                    res = jnp.where(chunk == g, pltpu.roll(rows[g], (32 * (g - q)) % 128, 1), res)
            store(4 * beta + q, res)


def swap_back(load, store):
    chunk = lax.broadcasted_iota(jnp.int32, (8, 128), 1) // 32
    for beta in range(3):
        rows = [load(4 * beta + q) for q in range(4)]
        for g in range(4):
            res = rows[g]
            for q in range(4):
                if g != q:
                    res = jnp.where(chunk == q, pltpu.roll(rows[q], (32 * (q - g)) % 128, 1), res)
            store(3 * g + beta, res)


def chunk_masks():
    chunk = lax.broadcasted_iota(jnp.int32, (16, 128), 1) // 32
    return [jnp.where(chunk == g, 1.0, 0.0).astype(jnp.bfloat16) for g in range(4)]


def fill_weights(weights):
    sub = lax.broadcasted_iota(jnp.int32, (8, 128), 0)
    zero = jnp.zeros((8, 128), jnp.float32)
    for n, k in ((2, 6), (3, 7)):
        one = jnp.where(sub == k, 1.0, 0.0)
        part = jnp.concatenate([one, zero], axis=0).astype(jnp.bfloat16)
        for g, mask in enumerate(chunk_masks()):
            for p in range(3):
                row = 64 * g + 16 * p
                weights[row:row + 16, 128 * n:128 * n + 128] = part * mask


def center_weights(rows, weights):
    sub = lax.broadcasted_iota(jnp.int32, (8, 128), 0)
    parts = pieces(rows)
    square, flow = products(rows)
    place = [jnp.where(sub < 3, -2.0 * p, 0.0) for p in parts]
    speed = [jnp.where(sub < 3, pltpu.roll(p, 5, 0), jnp.where(sub < 6, pltpu.roll(p, 3, 0), 0.0))
             for p in parts]

    def tail(lead, const):
        top, second, third = const
        return [jnp.where(sub == 6, top, jnp.where(sub == 7, second, lead)),
                jnp.where(sub == 0, third, 0.0)]

    def over(k):
        return [jnp.broadcast_to(p[k:k + 1], (8, 128)) for p in parts]
    masks = chunk_masks()
    tails = [tail(jnp.where(sub < 3, 1.0, 0.0), pieces(square)),
             tail(jnp.where((sub >= 3) & (sub < 6), -1.0, 0.0), pieces(-flow)),
             tail(jnp.zeros((8, 128), jnp.float32), over(6)),
             tail(jnp.zeros((8, 128), jnp.float32), over(7))]
    for n, last in enumerate(tails):
        blocks = [(3, last)]
        if n < 2:
            p = (place, speed)[n]
            blocks += [(0, p[:2]), (1, [p[0], p[2]]), (2, p[:2])]
        for at, part in blocks:
            part = jnp.concatenate(part, axis=0).astype(jnp.bfloat16)
            for g, mask in enumerate(masks):
                row = 64 * g + 16 * at
                weights[row:row + 16, 128 * n:128 * n + 128] = part * mask


def pair(drift, terms):
    r2, approach, dens, ratio = terms
    r2 = jnp.maximum(r2, 1e-30)
    support = jnp.maximum(1.0 - r2 * lax.rsqrt(r2), 0.0)
    slope = support * support * support
    visc = jnp.maximum(approach, 0.0) / ((r2 + visc_floor) * dens)
    return drift + slope * approach, (ratio + visc) * slope


def center_blocks(own, blocks):
    sub = lax.broadcasted_iota(jnp.int32, (8, 128), 0)

    def one(c, _):
        far_x = (c // 2).astype(jnp.float32) - 0.5
        far_y = (c % 2).astype(jnp.float32) - 0.5

        def store(r, vals):
            shift = jnp.where(sub == 0, far_x, jnp.where(sub == 1, far_y,
                              jnp.where(sub == 2, r - MIDDLE, 0.0)))
            blocks[c, r] = vals + shift
        swap_chunks(lambda r: own[c, r], store)
        return 0
    lax.fori_loop(0, 4, one, 0)


def all_pairs(blocks, lhs, places, bufs, forces, drifts, emit):
    chunk = lax.broadcasted_iota(jnp.int32, (8, 128), 1) // 32
    wide = lax.broadcasted_iota(jnp.int32, (64, 128), 1) // 32

    def first_column(c):
        return 4 * (c // 2) + c % 2

    def produce(n, weights, result):
        n = jnp.minimum(n, 4 * BLOCKS - 1)
        c, b = n // BLOCKS, n % BLOCKS
        center_weights(blocks[c, b], weights)
        rows = pl.ds(pl.multiple_of(32 * b, 32), 96)
        near = jnp.concatenate([lhs[first_column(c) + j, rows, :] for j in AROUND], axis=0)
        result[...] = jnp.dot(near, weights[...], preferred_element_type=jnp.float32)

    def consume(k, result):
        drift = jnp.zeros((8, 128), jnp.float32)
        for j in range(9):
            for d in range(3):
                for h in range(2):
                    both = []
                    for i in range(2):
                        r = 96 * j + 32 * d + 16 * h + 8 * i
                        terms = [result[r:r + 8, 128 * n:128 * n + 128] for n in range(4)]
                        drift, force = pair(drift, terms)
                        both.append(force)
                    full = jnp.concatenate(both, axis=0)
                    top = full.astype(jnp.bfloat16)
                    r = 128 * j + 32 * ((k - 1 + d) % 4) + 16 * h
                    forces[k, r:r + 16, 0:128] = top
                    forces[k, r:r + 16, 128:256] = (full - top.astype(jnp.float32)).astype(
                        jnp.bfloat16)
        drifts[k] = drift

    def reduce(n, k):
        n = jnp.maximum(n, 0)
        c, b = n // BLOCKS, n % BLOCKS
        tile = b // 4 + 1
        parts = []
        for j in AROUND:
            col = first_column(c) + j
            part = places[col, tile]
            if k == 0:
                part = jnp.where(wide == 3, places[col, tile - 1], part)
            if k == 3:
                part = jnp.where(wide == 0, places[col, tile + 1], part)
            parts.append(part)
        out = jnp.dot(jnp.concatenate(parts, axis=1), forces[k], preferred_element_type=jnp.float32)
        out = out[:, 0:128] + out[:, 128:256]
        first, second = out[0:8], out[8:16]
        for g in range(1, 4):
            first = jnp.where(chunk == g, out[16 * g:16 * g + 8], first)
            second = jnp.where(chunk == g, out[16 * g + 8:16 * g + 16], second)
        force = second[1:2]
        moments = [first[0:1] + first[3:4] + first[6:7], first[1:2] + first[4:5] + first[7:8],
                   first[2:3] + first[5:6] + second[0:1]]
        rows = blocks[c, b]
        sums = [rows[f:f + 1] * force - moments[f] for f in range(3)]
        sums.append(jnp.sum(drifts[k], axis=0, keepdims=True))
        emit(c, b, jnp.concatenate(sums + [jnp.zeros((4, 128), jnp.float32)], axis=0))

    fill_weights(bufs[0])
    fill_weights(bufs[2])
    produce(0, *bufs[:2])
    for k in range(4):
        for j in range(9):
            r = 128 * j + 32 * ((k + 2) % 4)
            forces[k, r:r + 32] = jnp.zeros((32, 256), jnp.bfloat16)

    def step(m, _):
        for k in range(UNROLL):
            consume(k % 4, bufs[2 * (k % 2) + 1])
            produce(UNROLL * m + k + 1, *bufs[2 * ((k + 1) % 2):2 * ((k + 1) % 2) + 2])
            reduce(UNROLL * m + k - 1, (k - 1) % 4)
        return 0
    lax.fori_loop(0, 4 * BLOCKS // UNROLL, step, 0)
    reduce(4 * BLOCKS - 1, 3)


def pass_kernel(final, base, own, slab_a, slab_b, tile_a, tile_b, out,
                cols, blocks, lhs, places, res, forces, drifts, *bufs):
    center_blocks(own, blocks)
    odd_s = lax.axis_index("slab") % 2
    odd_t = lax.axis_index("tile") % 2
    x_a, y_a = 3 - 3 * odd_s, 3 - 3 * odd_t
    x_b, y_b = 3 - x_a, 3 - y_a
    for i in range(2):
        for y in range(2):
            cols[4 * (i + 1) + y + 1] = own[2 * i + y]
        cols[4 * x_a + 1 + i] = slab_a[i]
        cols[4 * x_b + 1 + i] = slab_b[i]
    for ref, y in ((tile_a, y_a), (tile_b, y_b)):
        cols[4 * x_a + y] = ref[0]
        cols[4 + y] = ref[1]
        cols[8 + y] = ref[2]
        cols[4 * x_b + y] = ref[3]

    def one(j, _):
        column_features(cols.at[j], (j // 4).astype(jnp.float32) - 1.5,
                        (j % 4).astype(jnp.float32) - 1.5, j, lhs, places)
        return 0
    lax.fori_loop(0, 16, one, 0)

    def emit(c, b, sums):
        res[c, b] = sums
    all_pairs(blocks, lhs, places, bufs, forces, drifts, emit)

    def finish(c, _):
        def store(r, rates):
            now = base[c, r]
            present = now[6:7] != 0.0
            ax = -mass_grad * rates[0:1]
            ay = -mass_grad * rates[1:2]
            az = -mass_grad * rates[2:3] - gravity
            drift = -mass_grad * rates[3:4]
            half = 0.5 * time_step
            if not final:
                dens = now[6:7] + half * drift
                dens = jnp.where(present, dens, 1.0)
                ratio = eos_stiff * (dens**7 - 1.0) / (dens * dens)
                vals = [now[0:1] + half * now[3:4], now[1:2] + half * now[4:5],
                        now[2:3] + half * now[5:6], now[3:4] + half * ax,
                        now[4:5] + half * ay, now[5:6] + half * az, dens, ratio]
            else:
                v1 = [now[3:4] + time_step * ax, now[4:5] + time_step * ay,
                      now[5:6] + time_step * az]
                vals = [now[k:k + 1] + half * (now[3 + k:4 + k] + v1[k]) for k in range(3)]
                vals += v1 + [now[6:7] + time_step * drift, now[7:8]]
            full = jnp.concatenate(vals, axis=0)
            out[c, r] = jnp.where(jnp.broadcast_to(present, (8, 128)), full, 0.0)
        swap_back(lambda r: res[c, r], store)
        return 0
    lax.fori_loop(0, 4, finish, 0)


def swapped(value, axis, first):
    count = lax.axis_size(axis)
    trades = []
    for i in range(first, count - 1, 2):
        trades += [(i, i + 1), (i + 1, i)]
    return lax.ppermute(value, axis, trades)


def rates_pass(final, base, own):
    odd_s = lax.axis_index("slab") % 2
    odd_t = lax.axis_index("tile") % 2
    grid = own.reshape(2, 2, BLOCKS, 8, 128)
    slabs = [swapped(lax.dynamic_index_in_dim(grid, (1 - odd_s + k) % 2, 0, False), "slab", k)
             for k in range(2)]

    def edge(k):
        at = (1 - odd_t + k) % 2
        four = jnp.stack([slabs[0], grid[0], grid[1], slabs[1]])
        return lax.dynamic_index_in_dim(four, at, 1, False)
    tiles = [swapped(edge(k), "tile", k) for k in range(2)]

    def body(*refs):
        pass_kernel(final, *refs)
    work = [pltpu.VMEM((256, 512), jnp.bfloat16), pltpu.VMEM((864, 512), jnp.float32)]
    return pl.pallas_call(
        body,
        out_shape=jax.ShapeDtypeStruct((4, BLOCKS, 8, 128), jnp.float32),
        scratch_shapes=[pltpu.VMEM((16, BLOCKS, 8, 128), jnp.float32),
                        pltpu.VMEM((4, BLOCKS, 8, 128), jnp.float32),
                        pltpu.VMEM((16, SPAN, 256), jnp.bfloat16),
                        pltpu.VMEM((16, 5, 64, 128), jnp.bfloat16),
                        pltpu.VMEM((4, BLOCKS, 8, 128), jnp.float32),
                        pltpu.VMEM((4, 1152, 256), jnp.bfloat16),
                        pltpu.VMEM((4, 8, 128), jnp.float32),
                        *work, *work],
        compiler_params=pltpu.CompilerParams(vmem_limit_bytes=40 << 20),
        name="correct_pass" if final else "predict_pass",
    )(base, own, *slabs, *tiles)


def slot_mask(cell_counts):
    slot = lax.broadcasted_iota(jnp.int32, cell_counts.shape + (SLOTS,), cell_counts.ndim)
    return slot < cell_counts[..., None]


def pack_leavers(face_state, face_count, face_leave):
    cell_total = face_count.shape[0] * face_count.shape[1]
    row_total = cell_total * LMAX // 2
    leave_quota = face_leave.reshape(cell_total)
    occupancy = face_count.reshape(cell_total)
    row_ends = jnp.cumsum(leave_quota, dtype=jnp.int32)
    starts = row_ends - leave_quota
    row_ids = jnp.arange(row_total, dtype=jnp.int32)
    owner_mask = (starts[None, :] <= row_ids[:, None]) & (row_ends[None, :] > row_ids[:, None])
    root = jnp.arange(cell_total, dtype=jnp.int32) * SLOTS + occupancy - leave_quota - starts
    source_row = jnp.sum(jnp.where(owner_mask, root[None, :], 0), axis=1, dtype=jnp.int32) + row_ids
    flat_face = face_state.reshape(7, cell_total * SLOTS)
    return jnp.take(flat_face, source_row, axis=1)


def start_fields(particles, counts):
    mask = slot_mask(counts).reshape(2, 2, CZ * SLOTS)
    dens = jnp.where(mask, particles[6], 1.0)
    ratio = eos_stiff * (dens**7 - 1.0) / (dens * dens)
    fields = jnp.concatenate([particles, ratio[None]], axis=0)
    fields = jnp.where(mask[None], fields, 0.0)
    return fields.reshape(8, 4, BLOCKS, 128).transpose(1, 2, 0, 3)


def finish_fields(updated):
    return updated.transpose(2, 0, 1, 3)[:7].reshape(7, 2, 2, CZ * SLOTS)


def shards(particles, counts, leavers):
    fields = start_fields(particles, counts)
    middle = rates_pass(False, fields, fields)
    updated = finish_fields(rates_pass(True, fields, middle))
    remain = counts.at[0].add(-leavers[0, 0]).at[1].add(-leavers[1, 0])
    kept = jnp.where(slot_mask(remain).reshape(1, 2, 2, CZ * SLOTS), updated, 0.0)
    lower_rows = pack_leavers(updated[:, 0], counts[0], leavers[0, 0])
    upper_rows = pack_leavers(updated[:, 1], counts[1], leavers[1, 0])
    odd = lax.axis_index("slab") % 2 == 1
    first = swapped(jnp.where(odd, lower_rows, upper_rows), "slab", 0)
    second = swapped(jnp.where(odd, upper_rows, lower_rows), "slab", 1)
    return (kept, jnp.stack([jnp.where(odd, first, second), jnp.where(odd, second, first)]))


def solution(mesh):
    return jax.shard_map(
        shards,
        mesh=mesh,
        in_specs=(
            P(None, "slab", "tile", None),
            P("slab", "tile", None),
            P(None, "slab", "tile", None),
        ),
        out_specs=(P(None, "slab", "tile", None), P(None, None, ("slab", "tile"))),
        check_vma=False,
    )
```

```python
import math

import jax
import jax.numpy as jnp
from jax import lax
from jax.experimental import pallas as pl
from jax.experimental.pallas import tpu as pltpu
from jax.sharding import PartitionSpec as P

SLOTS = 32
LMAX = 4
FACE_ROWS = 192
CZ = 48
BLOCKS = 12

sound_speed = 10.0
smoothing = 0.5
kernel_norm = 21.0 / (16.0 * math.pi * smoothing**3)
grad_scale = -5.0 * kernel_norm / (smoothing * smoothing)
eos_stiff = sound_speed * sound_speed / 7.0
particle_mass = 0.125
viscosity = 0.1
visc_floor = 0.01 * smoothing * smoothing
time_step = 0.01
gravity = 9.81
mass_grad = particle_mass * grad_scale
visc_gain = 2.0 * viscosity * sound_speed * smoothing
FAR = 2.0**50
MIDDLE = 5.5
UNROLL = 12
SPAN = 32 * (BLOCKS + 2)
AROUND = (0, 1, 2, 4, 5, 6, 8, 9, 10)


def pieces(vals):
    top = vals.astype(jnp.bfloat16).astype(jnp.float32)
    rest = vals - top
    second = rest.astype(jnp.bfloat16).astype(jnp.float32)
    return top, second, rest - second


def products(vals):
    both = []
    for prod in (vals * vals, vals * pltpu.roll(vals, 5, 0)):
        rows = [jnp.broadcast_to(prod[k:k + 1], (8, 128)) for k in range(3)]
        both.append(rows[0] + rows[1] + rows[2])
    return both


def neighbour_rows(vals, far_x, far_y, far_z, sub):
    absent = jnp.broadcast_to(vals[6:7], (8, 128)) == 0.0
    shift = jnp.where(sub == 0, far_x, jnp.where(sub == 1, far_y, jnp.where(sub == 2, far_z, 0.0)))
    vals = jnp.where(absent, jnp.where(sub == 0, FAR, 0.0), vals + shift)
    high, mid, low = pieces(vals)
    square, flow = products(vals)
    tail = jnp.ones((8, 128), jnp.float32)
    for k, part in enumerate(pieces(square) + pieces(flow)):
        tail = jnp.where(sub == k, part, tail)
    last = jnp.where(sub == 0, 1.0, 0.0)
    turned = pltpu.roll(low, 6, 0)
    places = [jnp.where(sub < 3, high, jnp.where(sub < 6, pltpu.roll(mid, 3, 0), turned)),
              jnp.where(sub == 0, turned, jnp.where(sub == 1, 1.0, 0.0))]
    return [high, high, mid, high, low, mid, tail, last], places


def column_features(src, far_x, far_y, col, lhs, places):
    sub = lax.broadcasted_iota(jnp.int32, (8, 128), 0)
    chunk = lax.broadcasted_iota(jnp.int32, (8, 128), 1) // 32
    for beta in range(4):
        rows = []
        for g in range(4):
            if beta < 3:
                vals = src[3 * g + beta]
                level = (chunk + 4 * beta).astype(jnp.float32)
            else:
                none = jnp.zeros((8, 128), jnp.float32)
                below = src[3 * g - 1] if g > 0 else none
                above = src[3 * g + 3] if g < 3 else none
                vals = jnp.where(chunk == 3, below, jnp.where(chunk == 0, above, 0.0))
                level = jnp.where(chunk == 3, -1.0, 12.0)
            more, put = neighbour_rows(vals, far_x, far_y, level - MIDDLE, sub)
            rows += more
            put = jnp.concatenate(put, axis=0).astype(jnp.bfloat16)
            for tile in ((beta + 1,) if beta < 3 else (0, 4)):
                places[col, tile, 16 * g:16 * g + 16] = put
        for h in range(2):
            flat = jnp.concatenate(rows[16 * h:16 * h + 16], axis=0).T.astype(jnp.bfloat16)
            lanes = slice(128 * h, 128 * h + 128)
            if beta < 3:
                lhs[col, 128 * beta + 32:128 * beta + 160, lanes] = flat
            else:
                lhs[col, 0:32, lanes] = flat[96:128]
                lhs[col, 416:448, lanes] = flat[0:32]


def swap_chunks(load, store):
    chunk = lax.broadcasted_iota(jnp.int32, (8, 128), 1) // 32
    for beta in range(3):
        rows = [load(3 * g + beta) for g in range(4)]
        for q in range(4):
            res = rows[q]
            for g in range(4):
                if g != q:
                    res = jnp.where(chunk == g, pltpu.roll(rows[g], (32 * (g - q)) % 128, 1), res)
            store(4 * beta + q, res)


def swap_back(load, store):
    chunk = lax.broadcasted_iota(jnp.int32, (8, 128), 1) // 32
    for beta in range(3):
        rows = [load(4 * beta + q) for q in range(4)]
        for g in range(4):
            res = rows[g]
            for q in range(4):
                if g != q:
                    res = jnp.where(chunk == q, pltpu.roll(rows[q], (32 * (q - g)) % 128, 1), res)
            store(3 * g + beta, res)


def chunk_masks():
    chunk = lax.broadcasted_iota(jnp.int32, (16, 128), 1) // 32
    return [jnp.where(chunk == g, 1.0, 0.0).astype(jnp.bfloat16) for g in range(4)]


def fill_weights(weights):
    sub = lax.broadcasted_iota(jnp.int32, (8, 128), 0)
    zero = jnp.zeros((8, 128), jnp.float32)
    for n, k in ((2, 6), (3, 7)):
        one = jnp.where(sub == k, 1.0, 0.0)
        part = jnp.concatenate([one, zero], axis=0).astype(jnp.bfloat16)
        for g, mask in enumerate(chunk_masks()):
            for p in range(3):
                row = 64 * g + 16 * p
                weights[row:row + 16, 128 * n:128 * n + 128] = part * mask


def center_weights(rows, weights):
    sub = lax.broadcasted_iota(jnp.int32, (8, 128), 0)
    parts = pieces(rows)
    square, flow = products(rows)
    place = [jnp.where(sub < 3, -2.0 * p, 0.0) for p in parts]
    speed = [jnp.where(sub < 3, pltpu.roll(p, 5, 0), jnp.where(sub < 6, pltpu.roll(p, 3, 0), 0.0))
             for p in parts]

    def tail(lead, const):
        top, second, third = const
        return [jnp.where(sub == 6, top, jnp.where(sub == 7, second, lead)),
                jnp.where(sub == 0, third, 0.0)]

    def over(k):
        return [jnp.broadcast_to(p[k:k + 1], (8, 128)) for p in parts]
    masks = chunk_masks()
    tails = [tail(jnp.where(sub < 3, 1.0, 0.0), pieces(square)),
             tail(jnp.where((sub >= 3) & (sub < 6), -1.0, 0.0), pieces(-flow)),
             tail(jnp.zeros((8, 128), jnp.float32), over(6)),
             tail(jnp.zeros((8, 128), jnp.float32), over(7))]
    for n, last in enumerate(tails):
        blocks = [(3, last)]
        if n < 2:
            p = (place, speed)[n]
            blocks += [(0, p[:2]), (1, [p[0], p[2]]), (2, p[:2])]
        for at, part in blocks:
            part = jnp.concatenate(part, axis=0).astype(jnp.bfloat16)
            for g, mask in enumerate(masks):
                row = 64 * g + 16 * at
                weights[row:row + 16, 128 * n:128 * n + 128] = part * mask


def pair(drift, terms):
    r2, approach, dens, ratio = terms
    r2 = jnp.maximum(r2, 1e-30)
    support = jnp.maximum(1.0 - r2 * lax.rsqrt(r2), 0.0)
    slope = support * support * support
    visc = jnp.maximum(approach, 0.0) / ((r2 + visc_floor) * dens)
    return drift + slope * approach, (ratio + visc) * slope


def center_blocks(own, blocks):
    sub = lax.broadcasted_iota(jnp.int32, (8, 128), 0)

    def one(c, _):
        far_x = (c // 2).astype(jnp.float32) - 0.5
        far_y = (c % 2).astype(jnp.float32) - 0.5

        def store(r, vals):
            shift = jnp.where(sub == 0, far_x, jnp.where(sub == 1, far_y,
                              jnp.where(sub == 2, r - MIDDLE, 0.0)))
            blocks[c, r] = vals + shift
        swap_chunks(lambda r: own[c, r], store)
        return 0
    lax.fori_loop(0, 4, one, 0)


def all_pairs(blocks, lhs, places, bufs, forces, drifts, emit):
    chunk = lax.broadcasted_iota(jnp.int32, (8, 128), 1) // 32
    wide = lax.broadcasted_iota(jnp.int32, (64, 128), 1) // 32

    def first_column(c):
        return 4 * (c // 2) + c % 2

    def produce(n, weights, result):
        n = jnp.minimum(n, 4 * BLOCKS - 1)
        c, b = n // BLOCKS, n % BLOCKS
        center_weights(blocks[c, b], weights)
        rows = pl.ds(pl.multiple_of(32 * b, 32), 96)
        near = jnp.concatenate([lhs[first_column(c) + j, rows, :] for j in AROUND], axis=0)
        result[...] = jnp.dot(near, weights[...], preferred_element_type=jnp.float32)

    def consume(k, result):
        drift = jnp.zeros((8, 128), jnp.float32)
        for j in range(9):
            for d in range(3):
                for h in range(2):
                    both = []
                    for i in range(2):
                        r = 96 * j + 32 * d + 16 * h + 8 * i
                        terms = [result[r:r + 8, 128 * n:128 * n + 128] for n in range(4)]
                        drift, force = pair(drift, terms)
                        both.append(force)
                    full = jnp.concatenate(both, axis=0)
                    top = full.astype(jnp.bfloat16)
                    r = 128 * j + 32 * ((k - 1 + d) % 4) + 16 * h
                    forces[k, r:r + 16, 0:128] = top
                    forces[k, r:r + 16, 128:256] = (full - top.astype(jnp.float32)).astype(
                        jnp.bfloat16)
        drifts[k] = drift

    def reduce(n, k):
        n = jnp.maximum(n, 0)
        c, b = n // BLOCKS, n % BLOCKS
        tile = b // 4 + 1
        parts = []
        for j in AROUND:
            col = first_column(c) + j
            part = places[col, tile]
            if k == 0:
                part = jnp.where(wide == 3, places[col, tile - 1], part)
            if k == 3:
                part = jnp.where(wide == 0, places[col, tile + 1], part)
            parts.append(part)
        out = jnp.dot(jnp.concatenate(parts, axis=1), forces[k], preferred_element_type=jnp.float32)
        out = out[:, 0:128] + out[:, 128:256]
        first, second = out[0:8], out[8:16]
        for g in range(1, 4):
            first = jnp.where(chunk == g, out[16 * g:16 * g + 8], first)
            second = jnp.where(chunk == g, out[16 * g + 8:16 * g + 16], second)
        force = second[1:2]
        moments = [first[0:1] + first[3:4] + first[6:7], first[1:2] + first[4:5] + first[7:8],
                   first[2:3] + first[5:6] + second[0:1]]
        rows = blocks[c, b]
        sums = [rows[f:f + 1] * force - moments[f] for f in range(3)]
        sums.append(jnp.sum(drifts[k], axis=0, keepdims=True))
        emit(c, b, jnp.concatenate(sums + [jnp.zeros((4, 128), jnp.float32)], axis=0))

    fill_weights(bufs[0])
    fill_weights(bufs[2])
    produce(0, *bufs[:2])
    for k in range(4):
        for j in range(9):
            r = 128 * j + 32 * ((k + 2) % 4)
            forces[k, r:r + 32] = jnp.zeros((32, 256), jnp.bfloat16)

    def step(m, _):
        for k in range(UNROLL):
            consume(k % 4, bufs[2 * (k % 2) + 1])
            produce(UNROLL * m + k + 1, *bufs[2 * ((k + 1) % 2):2 * ((k + 1) % 2) + 2])
            reduce(UNROLL * m + k - 1, (k - 1) % 4)
        return 0
    lax.fori_loop(0, 4 * BLOCKS // UNROLL, step, 0)
    reduce(4 * BLOCKS - 1, 3)


def leaving(fields, x, source):
    number = lax.broadcasted_iota(jnp.int32, (256, 256), 0)
    source = jnp.broadcast_to(source[0:1], (256, 256))
    total = jnp.zeros((32, 256), jnp.float32)
    for y in range(2):
        for h in range(6):
            vals = jnp.concatenate([fields[2 * x + y, 2 * h], fields[2 * x + y, 2 * h + 1]], axis=1)
            rows = jnp.concatenate([*pieces(vals), jnp.zeros((8, 256), jnp.float32)], axis=0)
            hit = jnp.where(number == source - 256 * (6 * y + h), 1.0, 0.0)
            total = total + jnp.dot(rows.astype(jnp.bfloat16), hit.astype(jnp.bfloat16),
                                    preferred_element_type=jnp.float32)
    return (total[0:8] + total[8:16] + total[16:24])[:7, :FACE_ROWS]


def pass_kernel(final, base, own, slab_a, slab_b, tile_a, tile_b, sources, outs,
                cols, blocks, lhs, places, res, forces, drifts, *bufs):
    out = outs[0]
    center_blocks(own, blocks)
    odd_s = lax.axis_index("slab") % 2
    odd_t = lax.axis_index("tile") % 2
    x_a, y_a = 3 - 3 * odd_s, 3 - 3 * odd_t
    x_b, y_b = 3 - x_a, 3 - y_a
    for i in range(2):
        for y in range(2):
            cols[4 * (i + 1) + y + 1] = own[2 * i + y]
        cols[4 * x_a + 1 + i] = slab_a[i]
        cols[4 * x_b + 1 + i] = slab_b[i]
    for ref, y in ((tile_a, y_a), (tile_b, y_b)):
        cols[4 * x_a + y] = ref[0]
        cols[4 + y] = ref[1]
        cols[8 + y] = ref[2]
        cols[4 * x_b + y] = ref[3]

    def one(j, _):
        column_features(cols.at[j], (j // 4).astype(jnp.float32) - 1.5,
                        (j % 4).astype(jnp.float32) - 1.5, j, lhs, places)
        return 0
    lax.fori_loop(0, 16, one, 0)

    def emit(c, b, sums):
        res[c, b] = sums
    all_pairs(blocks, lhs, places, bufs, forces, drifts, emit)

    def finish(c, _):
        def store(r, rates):
            now = base[c, r]
            present = now[6:7] != 0.0
            ax = -mass_grad * rates[0:1]
            ay = -mass_grad * rates[1:2]
            az = -mass_grad * rates[2:3] - gravity
            drift = -mass_grad * rates[3:4]
            half = 0.5 * time_step
            if not final:
                dens = now[6:7] + half * drift
                dens = jnp.where(present, dens, 1.0)
                ratio = eos_stiff * (dens**7 - 1.0) / (dens * dens)
                vals = [now[0:1] + half * now[3:4], now[1:2] + half * now[4:5],
                        now[2:3] + half * now[5:6], now[3:4] + half * ax,
                        now[4:5] + half * ay, now[5:6] + half * az, dens, ratio]
            else:
                v1 = [now[3:4] + time_step * ax, now[4:5] + time_step * ay,
                      now[5:6] + time_step * az]
                vals = [now[k:k + 1] + half * (now[3 + k:4 + k] + v1[k]) for k in range(3)]
                vals += v1 + [now[6:7] + time_step * drift, now[7:8]]
            full = jnp.concatenate(vals, axis=0)
            out[c, r] = jnp.where(jnp.broadcast_to(present, (8, 128)), full, 0.0)
        swap_back(lambda r: res[c, r], store)
        return 0
    lax.fori_loop(0, 4, finish, 0)
    for k in range(2):
        x = (1 - odd_s + k) % 2
        if final:
            outs[1 + k][...] = leaving(out, x, sources[0][x])
        else:
            for y in range(2):
                outs[1 + k][y] = out[2 * x + y]


def swapped(value, axis, first):
    count = lax.axis_size(axis)
    trades = []
    for i in range(first, count - 1, 2):
        trades += [(i, i + 1), (i + 1, i)]
    return lax.ppermute(value, axis, trades)


def rates_pass(final, base, own, faces, extra=()):
    odd_t = lax.axis_index("tile") % 2
    grid = own.reshape(2, 2, BLOCKS, 8, 128)
    slabs = [swapped(faces[k], "slab", k) for k in range(2)]

    def edge(k):
        at = (1 - odd_t + k) % 2
        four = jnp.stack([slabs[0], grid[0], grid[1], slabs[1]])
        return lax.dynamic_index_in_dim(four, at, 1, False)
    tiles = [swapped(edge(k), "tile", k) for k in range(2)]

    ins = 6 + len(extra)

    def body(*refs):
        pass_kernel(final, *refs[:6], refs[6:ins], refs[ins:ins + 3], *refs[ins + 3:])
    whole = jax.ShapeDtypeStruct((4, BLOCKS, 8, 128), jnp.float32)
    face = jax.ShapeDtypeStruct((7, FACE_ROWS) if final else (2, BLOCKS, 8, 128), jnp.float32)
    work = [pltpu.VMEM((256, 512), jnp.bfloat16), pltpu.VMEM((864, 512), jnp.float32)]
    return pl.pallas_call(
        body,
        out_shape=(whole, face, face),
        scratch_shapes=[pltpu.VMEM((16, BLOCKS, 8, 128), jnp.float32),
                        pltpu.VMEM((4, BLOCKS, 8, 128), jnp.float32),
                        pltpu.VMEM((16, SPAN, 256), jnp.bfloat16),
                        pltpu.VMEM((16, 5, 64, 128), jnp.bfloat16),
                        pltpu.VMEM((4, BLOCKS, 8, 128), jnp.float32),
                        pltpu.VMEM((4, 1152, 256), jnp.bfloat16),
                        pltpu.VMEM((4, 8, 128), jnp.float32),
                        *work, *work],
        compiler_params=pltpu.CompilerParams(vmem_limit_bytes=40 << 20),
        name="correct_pass" if final else "predict_pass",
    )(base, own, *slabs, *tiles, *extra)


def slot_mask(cell_counts):
    slot = lax.broadcasted_iota(jnp.int32, cell_counts.shape + (SLOTS,), cell_counts.ndim)
    return slot < cell_counts[..., None]


def leaver_sources(face_count, face_leave):
    cell_total = face_count.shape[0] * face_count.shape[1]
    leave_quota = face_leave.reshape(cell_total)
    occupancy = face_count.reshape(cell_total)
    row_ends = jnp.cumsum(leave_quota, dtype=jnp.int32)
    starts = row_ends - leave_quota
    row_ids = jnp.arange(FACE_ROWS, dtype=jnp.int32)
    owner_mask = (starts[None, :] <= row_ids[:, None]) & (row_ends[None, :] > row_ids[:, None])
    root = jnp.arange(cell_total, dtype=jnp.int32) * SLOTS + occupancy - leave_quota - starts
    source_row = jnp.sum(jnp.where(owner_mask, root[None, :], 0), axis=1, dtype=jnp.int32) + row_ids
    return jnp.pad(source_row, (0, 256 - FACE_ROWS), constant_values=-1)


def start_fields(particles, counts):
    mask = slot_mask(counts).reshape(2, 2, CZ * SLOTS)
    dens = jnp.where(mask, particles[6], 1.0)
    ratio = eos_stiff * (dens**7 - 1.0) / (dens * dens)
    fields = jnp.concatenate([particles, ratio[None]], axis=0)
    fields = jnp.where(mask[None], fields, 0.0)
    return fields.reshape(8, 4, BLOCKS, 128).transpose(1, 2, 0, 3)


def finish_fields(updated):
    return updated.transpose(2, 0, 1, 3)[:7].reshape(7, 2, 2, CZ * SLOTS)


def shards(particles, counts, leavers):
    fields = start_fields(particles, counts)
    odd = lax.axis_index("slab") % 2
    grid = fields.reshape(2, 2, BLOCKS, 8, 128)
    faces = [lax.dynamic_index_in_dim(grid, (1 - odd + k) % 2, 0, False) for k in range(2)]
    middle, *faces = rates_pass(False, fields, fields, faces)
    sources = jnp.stack([leaver_sources(counts[k], leavers[k, 0]) for k in range(2)])
    sources = jnp.broadcast_to(sources[:, None], (2, 8, 256))
    updated, *rows = rates_pass(True, fields, middle, faces, (sources,))
    updated = finish_fields(updated)
    remain = counts.at[0].add(-leavers[0, 0]).at[1].add(-leavers[1, 0])
    kept = jnp.where(slot_mask(remain).reshape(1, 2, 2, CZ * SLOTS), updated, 0.0)
    first, second = swapped(rows[0], "slab", 0), swapped(rows[1], "slab", 1)
    odd = odd == 1
    return (kept, jnp.stack([jnp.where(odd, first, second), jnp.where(odd, second, first)]))


def solution(mesh):
    return jax.shard_map(
        shards,
        mesh=mesh,
        in_specs=(
            P(None, "slab", "tile", None),
            P("slab", "tile", None),
            P(None, "slab", "tile", None),
        ),
        out_specs=(P(None, "slab", "tile", None), P(None, None, ("slab", "tile"))),
        check_vma=False,
    )
```

```python
import math

import jax
import jax.numpy as jnp
from jax import lax
from jax.experimental import pallas as pl
from jax.experimental.pallas import tpu as pltpu
from jax.sharding import PartitionSpec as P

SLOTS = 32
LMAX = 4
FACE_ROWS = 192
CZ = 48
BLOCKS = 12

sound_speed = 10.0
smoothing = 0.5
kernel_norm = 21.0 / (16.0 * math.pi * smoothing**3)
grad_scale = -5.0 * kernel_norm / (smoothing * smoothing)
eos_stiff = sound_speed * sound_speed / 7.0
particle_mass = 0.125
viscosity = 0.1
visc_floor = 0.01 * smoothing * smoothing
time_step = 0.01
gravity = 9.81
mass_grad = particle_mass * grad_scale
visc_gain = 2.0 * viscosity * sound_speed * smoothing
FAR = 2.0**50
MIDDLE = 5.5
UNROLL = 24
SPAN = 32 * (BLOCKS + 2)
AROUND = (0, 1, 2, 4, 5, 6, 8, 9, 10)


def pieces(vals):
    top = vals.astype(jnp.bfloat16).astype(jnp.float32)
    rest = vals - top
    second = rest.astype(jnp.bfloat16).astype(jnp.float32)
    return top, second, rest - second


def products(vals):
    both = []
    for prod in (vals * vals, vals * pltpu.roll(vals, 5, 0)):
        rows = [jnp.broadcast_to(prod[k:k + 1], (8, 128)) for k in range(3)]
        both.append(rows[0] + rows[1] + rows[2])
    return both


def neighbour_rows(vals, far_x, far_y, far_z, sub):
    absent = jnp.broadcast_to(vals[6:7], (8, 128)) == 0.0
    shift = jnp.where(sub == 0, far_x, jnp.where(sub == 1, far_y, jnp.where(sub == 2, far_z, 0.0)))
    vals = jnp.where(absent, jnp.where(sub == 0, FAR, 0.0), vals + shift)
    high, mid, low = pieces(vals)
    square, flow = products(vals)
    tail = jnp.ones((8, 128), jnp.float32)
    for k, part in enumerate(pieces(square) + pieces(flow)):
        tail = jnp.where(sub == k, part, tail)
    last = jnp.where(sub == 0, 1.0, 0.0)
    turned = pltpu.roll(low, 6, 0)
    places = [jnp.where(sub < 3, high, jnp.where(sub < 6, pltpu.roll(mid, 3, 0), turned)),
              jnp.where(sub == 0, turned, jnp.where(sub == 1, 1.0, 0.0))]
    return [high, high, mid, high, low, mid, tail, last], places


def column_features(src, far_x, far_y, col, lhs, places):
    sub = lax.broadcasted_iota(jnp.int32, (8, 128), 0)
    chunk = lax.broadcasted_iota(jnp.int32, (8, 128), 1) // 32
    for beta in range(4):
        rows = []
        for g in range(4):
            if beta < 3:
                vals = src[3 * g + beta]
                level = (chunk + 4 * beta).astype(jnp.float32)
            else:
                none = jnp.zeros((8, 128), jnp.float32)
                below = src[3 * g - 1] if g > 0 else none
                above = src[3 * g + 3] if g < 3 else none
                vals = jnp.where(chunk == 3, below, jnp.where(chunk == 0, above, 0.0))
                level = jnp.where(chunk == 3, -1.0, 12.0)
            more, put = neighbour_rows(vals, far_x, far_y, level - MIDDLE, sub)
            rows += more
            put = jnp.concatenate(put, axis=0).astype(jnp.bfloat16)
            for tile in ((beta + 1,) if beta < 3 else (0, 4)):
                places[col, tile, 16 * g:16 * g + 16] = put
        for h in range(2):
            flat = jnp.concatenate(rows[16 * h:16 * h + 16], axis=0).T.astype(jnp.bfloat16)
            lanes = slice(128 * h, 128 * h + 128)
            if beta < 3:
                lhs[col, 128 * beta + 32:128 * beta + 160, lanes] = flat
            else:
                lhs[col, 0:32, lanes] = flat[96:128]
                lhs[col, 416:448, lanes] = flat[0:32]


def swap_chunks(load, store):
    chunk = lax.broadcasted_iota(jnp.int32, (8, 128), 1) // 32
    for beta in range(3):
        rows = [load(3 * g + beta) for g in range(4)]
        for q in range(4):
            res = rows[q]
            for g in range(4):
                if g != q:
                    res = jnp.where(chunk == g, pltpu.roll(rows[g], (32 * (g - q)) % 128, 1), res)
            store(4 * beta + q, res)


def swap_back(load, store):
    chunk = lax.broadcasted_iota(jnp.int32, (8, 128), 1) // 32
    for beta in range(3):
        rows = [load(4 * beta + q) for q in range(4)]
        for g in range(4):
            res = rows[g]
            for q in range(4):
                if g != q:
                    res = jnp.where(chunk == q, pltpu.roll(rows[q], (32 * (q - g)) % 128, 1), res)
            store(3 * g + beta, res)


def chunk_masks():
    chunk = lax.broadcasted_iota(jnp.int32, (16, 128), 1) // 32
    return [jnp.where(chunk == g, 1.0, 0.0).astype(jnp.bfloat16) for g in range(4)]


def fill_weights(weights):
    sub = lax.broadcasted_iota(jnp.int32, (8, 128), 0)
    zero = jnp.zeros((8, 128), jnp.float32)
    for n, k in ((2, 6), (3, 7)):
        one = jnp.where(sub == k, 1.0, 0.0)
        part = jnp.concatenate([one, zero], axis=0).astype(jnp.bfloat16)
        for g, mask in enumerate(chunk_masks()):
            for p in range(3):
                row = 64 * g + 16 * p
                weights[row:row + 16, 128 * n:128 * n + 128] = part * mask


def center_weights(rows, weights):
    sub = lax.broadcasted_iota(jnp.int32, (8, 128), 0)
    parts = pieces(rows)
    square, flow = products(rows)
    place = [jnp.where(sub < 3, -2.0 * p, 0.0) for p in parts]
    speed = [jnp.where(sub < 3, pltpu.roll(p, 5, 0), jnp.where(sub < 6, pltpu.roll(p, 3, 0), 0.0))
             for p in parts]

    def tail(lead, const):
        top, second, third = const
        return [jnp.where(sub == 6, top, jnp.where(sub == 7, second, lead)),
                jnp.where(sub == 0, third, 0.0)]

    def over(k):
        return [jnp.broadcast_to(p[k:k + 1], (8, 128)) for p in parts]
    masks = chunk_masks()
    tails = [tail(jnp.where(sub < 3, 1.0, 0.0), pieces(square)),
             tail(jnp.where((sub >= 3) & (sub < 6), -1.0, 0.0), pieces(-flow)),
             tail(jnp.zeros((8, 128), jnp.float32), over(6)),
             tail(jnp.zeros((8, 128), jnp.float32), over(7))]
    for n, last in enumerate(tails):
        blocks = [(3, last)]
        if n < 2:
            p = (place, speed)[n]
            blocks += [(0, p[:2]), (1, [p[0], p[2]]), (2, p[:2])]
        for at, part in blocks:
            part = jnp.concatenate(part, axis=0).astype(jnp.bfloat16)
            for g, mask in enumerate(masks):
                row = 64 * g + 16 * at
                weights[row:row + 16, 128 * n:128 * n + 128] = part * mask


def pair(drift, terms):
    r2, approach, dens, ratio = terms
    r2 = jnp.maximum(r2, 1e-30)
    support = jnp.maximum(1.0 - r2 * lax.rsqrt(r2), 0.0)
    slope = support * support * support
    visc = jnp.maximum(approach, 0.0) / ((r2 + visc_floor) * dens)
    return drift + slope * approach, (ratio + visc) * slope


def center_blocks(own, blocks):
    sub = lax.broadcasted_iota(jnp.int32, (8, 128), 0)

    def one(c, _):
        far_x = (c // 2).astype(jnp.float32) - 0.5
        far_y = (c % 2).astype(jnp.float32) - 0.5

        def store(r, vals):
            shift = jnp.where(sub == 0, far_x, jnp.where(sub == 1, far_y,
                              jnp.where(sub == 2, r - MIDDLE, 0.0)))
            blocks[c, r] = vals + shift
        swap_chunks(lambda r: own[c, r], store)
        return 0
    lax.fori_loop(0, 4, one, 0)


def all_pairs(blocks, lhs, places, bufs, forces, drifts, emit):
    chunk = lax.broadcasted_iota(jnp.int32, (8, 128), 1) // 32
    wide = lax.broadcasted_iota(jnp.int32, (64, 128), 1) // 32

    def first_column(c):
        return 4 * (c // 2) + c % 2

    def produce(n, weights, result):
        n = jnp.minimum(n, 4 * BLOCKS - 1)
        c, b = n // BLOCKS, n % BLOCKS
        center_weights(blocks[c, b], weights)
        rows = pl.ds(pl.multiple_of(32 * b, 32), 96)
        near = jnp.concatenate([lhs[first_column(c) + j, rows, :] for j in AROUND], axis=0)
        result[...] = jnp.dot(near, weights[...], preferred_element_type=jnp.float32)

    def consume(k, result):
        drift = jnp.zeros((8, 128), jnp.float32)
        for j in range(9):
            for d in range(3):
                for h in range(2):
                    both = []
                    for i in range(2):
                        r = 96 * j + 32 * d + 16 * h + 8 * i
                        terms = [result[r:r + 8, 128 * n:128 * n + 128] for n in range(4)]
                        drift, force = pair(drift, terms)
                        both.append(force)
                    full = jnp.concatenate(both, axis=0)
                    top = full.astype(jnp.bfloat16)
                    r = 128 * j + 32 * ((k - 1 + d) % 4) + 16 * h
                    forces[k, r:r + 16, 0:128] = top
                    forces[k, r:r + 16, 128:256] = (full - top.astype(jnp.float32)).astype(
                        jnp.bfloat16)
        drifts[k] = drift

    def reduce(n, k):
        n = jnp.maximum(n, 0)
        c, b = n // BLOCKS, n % BLOCKS
        tile = b // 4 + 1
        parts = []
        for j in AROUND:
            col = first_column(c) + j
            part = places[col, tile]
            if k == 0:
                part = jnp.where(wide == 3, places[col, tile - 1], part)
            if k == 3:
                part = jnp.where(wide == 0, places[col, tile + 1], part)
            parts.append(part)
        out = jnp.dot(jnp.concatenate(parts, axis=1), forces[k], preferred_element_type=jnp.float32)
        out = out[:, 0:128] + out[:, 128:256]
        first, second = out[0:8], out[8:16]
        for g in range(1, 4):
            first = jnp.where(chunk == g, out[16 * g:16 * g + 8], first)
            second = jnp.where(chunk == g, out[16 * g + 8:16 * g + 16], second)
        force = second[1:2]
        moments = [first[0:1] + first[3:4] + first[6:7], first[1:2] + first[4:5] + first[7:8],
                   first[2:3] + first[5:6] + second[0:1]]
        rows = blocks[c, b]
        sums = [rows[f:f + 1] * force - moments[f] for f in range(3)]
        sums.append(jnp.sum(drifts[k], axis=0, keepdims=True))
        emit(c, b, jnp.concatenate(sums + [jnp.zeros((4, 128), jnp.float32)], axis=0))

    fill_weights(bufs[0])
    fill_weights(bufs[2])
    produce(0, *bufs[:2])
    for k in range(4):
        for j in range(9):
            r = 128 * j + 32 * ((k + 2) % 4)
            forces[k, r:r + 32] = jnp.zeros((32, 256), jnp.bfloat16)

    def step(m, _):
        for k in range(UNROLL):
            consume(k % 4, bufs[2 * (k % 2) + 1])
            produce(UNROLL * m + k + 1, *bufs[2 * ((k + 1) % 2):2 * ((k + 1) % 2) + 2])
            reduce(UNROLL * m + k - 1, (k - 1) % 4)
        return 0
    lax.fori_loop(0, 4 * BLOCKS // UNROLL, step, 0)
    reduce(4 * BLOCKS - 1, 3)


def leaving(fields, x, source):
    number = lax.broadcasted_iota(jnp.int32, (256, 256), 0)
    source = jnp.broadcast_to(source[0:1], (256, 256))
    total = jnp.zeros((32, 256), jnp.float32)
    for y in range(2):
        for h in range(6):
            vals = jnp.concatenate([fields[2 * x + y, 2 * h], fields[2 * x + y, 2 * h + 1]], axis=1)
            rows = jnp.concatenate([*pieces(vals), jnp.zeros((8, 256), jnp.float32)], axis=0)
            hit = jnp.where(number == source - 256 * (6 * y + h), 1.0, 0.0)
            total = total + jnp.dot(rows.astype(jnp.bfloat16), hit.astype(jnp.bfloat16),
                                    preferred_element_type=jnp.float32)
    return (total[0:8] + total[8:16] + total[16:24])[:7, :FACE_ROWS]


def pass_kernel(final, base, own, slab_a, slab_b, tile_a, tile_b, sources, outs,
                cols, blocks, lhs, places, res, forces, drifts, *bufs):
    out = outs[0]
    center_blocks(own, blocks)
    odd_s = lax.axis_index("slab") % 2
    odd_t = lax.axis_index("tile") % 2
    x_a, y_a = 3 - 3 * odd_s, 3 - 3 * odd_t
    x_b, y_b = 3 - x_a, 3 - y_a
    for i in range(2):
        for y in range(2):
            cols[4 * (i + 1) + y + 1] = own[2 * i + y]
        cols[4 * x_a + 1 + i] = slab_a[i]
        cols[4 * x_b + 1 + i] = slab_b[i]
    for ref, y in ((tile_a, y_a), (tile_b, y_b)):
        cols[4 * x_a + y] = ref[0]
        cols[4 + y] = ref[1]
        cols[8 + y] = ref[2]
        cols[4 * x_b + y] = ref[3]

    def one(j, _):
        column_features(cols.at[j], (j // 4).astype(jnp.float32) - 1.5,
                        (j % 4).astype(jnp.float32) - 1.5, j, lhs, places)
        return 0
    lax.fori_loop(0, 16, one, 0)

    def emit(c, b, sums):
        res[c, b] = sums
    all_pairs(blocks, lhs, places, bufs, forces, drifts, emit)

    def finish(c, _):
        def store(r, rates):
            now = base[c, r]
            present = now[6:7] != 0.0
            ax = -mass_grad * rates[0:1]
            ay = -mass_grad * rates[1:2]
            az = -mass_grad * rates[2:3] - gravity
            drift = -mass_grad * rates[3:4]
            half = 0.5 * time_step
            if not final:
                dens = now[6:7] + half * drift
                dens = jnp.where(present, dens, 1.0)
                ratio = eos_stiff * (dens**7 - 1.0) / (dens * dens)
                vals = [now[0:1] + half * now[3:4], now[1:2] + half * now[4:5],
                        now[2:3] + half * now[5:6], now[3:4] + half * ax,
                        now[4:5] + half * ay, now[5:6] + half * az, dens, ratio]
            else:
                v1 = [now[3:4] + time_step * ax, now[4:5] + time_step * ay,
                      now[5:6] + time_step * az]
                vals = [now[k:k + 1] + half * (now[3 + k:4 + k] + v1[k]) for k in range(3)]
                vals += v1 + [now[6:7] + time_step * drift, now[7:8]]
            full = jnp.concatenate(vals, axis=0)
            out[c, r] = jnp.where(jnp.broadcast_to(present, (8, 128)), full, 0.0)
        swap_back(lambda r: res[c, r], store)
        return 0
    lax.fori_loop(0, 4, finish, 0)
    for k in range(2):
        x = (1 - odd_s + k) % 2
        if final:
            outs[1 + k][...] = leaving(out, x, sources[0][x])
        else:
            for y in range(2):
                outs[1 + k][y] = out[2 * x + y]


def swapped(value, axis, first):
    count = lax.axis_size(axis)
    trades = []
    for i in range(first, count - 1, 2):
        trades += [(i, i + 1), (i + 1, i)]
    return lax.ppermute(value, axis, trades)


def rates_pass(final, base, own, faces, extra=()):
    odd_t = lax.axis_index("tile") % 2
    grid = own.reshape(2, 2, BLOCKS, 8, 128)
    slabs = [swapped(faces[k], "slab", k) for k in range(2)]

    def edge(k):
        at = (1 - odd_t + k) % 2
        four = jnp.stack([slabs[0], grid[0], grid[1], slabs[1]])
        return lax.dynamic_index_in_dim(four, at, 1, False)
    tiles = [swapped(edge(k), "tile", k) for k in range(2)]

    ins = 6 + len(extra)

    def body(*refs):
        pass_kernel(final, *refs[:6], refs[6:ins], refs[ins:ins + 3], *refs[ins + 3:])
    whole = jax.ShapeDtypeStruct((4, BLOCKS, 8, 128), jnp.float32)
    face = jax.ShapeDtypeStruct((7, FACE_ROWS) if final else (2, BLOCKS, 8, 128), jnp.float32)
    work = [pltpu.VMEM((256, 512), jnp.bfloat16), pltpu.VMEM((864, 512), jnp.float32)]
    return pl.pallas_call(
        body,
        out_shape=(whole, face, face),
        scratch_shapes=[pltpu.VMEM((16, BLOCKS, 8, 128), jnp.float32),
                        pltpu.VMEM((4, BLOCKS, 8, 128), jnp.float32),
                        pltpu.VMEM((16, SPAN, 256), jnp.bfloat16),
                        pltpu.VMEM((16, 5, 64, 128), jnp.bfloat16),
                        pltpu.VMEM((4, BLOCKS, 8, 128), jnp.float32),
                        pltpu.VMEM((4, 1152, 256), jnp.bfloat16),
                        pltpu.VMEM((4, 8, 128), jnp.float32),
                        *work, *work],
        compiler_params=pltpu.CompilerParams(vmem_limit_bytes=40 << 20),
        name="correct_pass" if final else "predict_pass",
    )(base, own, *slabs, *tiles, *extra)


def slot_mask(cell_counts):
    slot = lax.broadcasted_iota(jnp.int32, cell_counts.shape + (SLOTS,), cell_counts.ndim)
    return slot < cell_counts[..., None]


def leaver_sources(face_count, face_leave):
    cell_total = face_count.shape[0] * face_count.shape[1]
    leave_quota = face_leave.reshape(cell_total)
    occupancy = face_count.reshape(cell_total)
    row_ends = jnp.cumsum(leave_quota, dtype=jnp.int32)
    starts = row_ends - leave_quota
    row_ids = jnp.arange(FACE_ROWS, dtype=jnp.int32)
    owner_mask = (starts[None, :] <= row_ids[:, None]) & (row_ends[None, :] > row_ids[:, None])
    root = jnp.arange(cell_total, dtype=jnp.int32) * SLOTS + occupancy - leave_quota - starts
    source_row = jnp.sum(jnp.where(owner_mask, root[None, :], 0), axis=1, dtype=jnp.int32) + row_ids
    return jnp.pad(source_row, (0, 256 - FACE_ROWS), constant_values=-1)


def start_fields(particles, counts):
    mask = slot_mask(counts).reshape(2, 2, CZ * SLOTS)
    dens = jnp.where(mask, particles[6], 1.0)
    ratio = eos_stiff * (dens**7 - 1.0) / (dens * dens)
    fields = jnp.concatenate([particles, ratio[None]], axis=0)
    fields = jnp.where(mask[None], fields, 0.0)
    return fields.reshape(8, 4, BLOCKS, 128).transpose(1, 2, 0, 3)


def finish_fields(updated):
    return updated.transpose(2, 0, 1, 3)[:7].reshape(7, 2, 2, CZ * SLOTS)


def shards(particles, counts, leavers):
    fields = start_fields(particles, counts)
    odd = lax.axis_index("slab") % 2
    grid = fields.reshape(2, 2, BLOCKS, 8, 128)
    faces = [lax.dynamic_index_in_dim(grid, (1 - odd + k) % 2, 0, False) for k in range(2)]
    middle, *faces = rates_pass(False, fields, fields, faces)
    sources = jnp.stack([leaver_sources(counts[k], leavers[k, 0]) for k in range(2)])
    sources = jnp.broadcast_to(sources[:, None], (2, 8, 256))
    updated, *rows = rates_pass(True, fields, middle, faces, (sources,))
    updated = finish_fields(updated)
    remain = counts.at[0].add(-leavers[0, 0]).at[1].add(-leavers[1, 0])
    kept = jnp.where(slot_mask(remain).reshape(1, 2, 2, CZ * SLOTS), updated, 0.0)
    first, second = swapped(rows[0], "slab", 0), swapped(rows[1], "slab", 1)
    odd = odd == 1
    return (kept, jnp.stack([jnp.where(odd, first, second), jnp.where(odd, second, first)]))


def solution(mesh):
    return jax.shard_map(
        shards,
        mesh=mesh,
        in_specs=(
            P(None, "slab", "tile", None),
            P("slab", "tile", None),
            P(None, "slab", "tile", None),
        ),
        out_specs=(P(None, "slab", "tile", None), P(None, None, ("slab", "tile"))),
        check_vma=False,
    )
```
